768 devices in a mesh: gz: 96 (over y, z), ta: 8 (over x, core).
Axes of the slice: x: 4, y: 8, z: 12, core: 2. Of those that a mesh axis runs over, the one named last changes fastest.
Arguments:
- log_mean: float32 [96, 512, 512], P('gz', 'ta'), may hold values from -6 to 6
- tile_mask: int32 [96, 512, 512], P('gz', 'ta'), may hold values 0 or 1
- coverage: int32 [96, 512, 512], P('gz', 'ta'), may hold values from 0 to 4096
- lifetime: float32 [512, 512], P('ta'), may hold values from 0 to 40, as said below
- keep: float32 [96], replicated, may hold values from 0 to 1, as said below
Outputs:
- corrected: float32 [96, 512, 512], P('gz', None, 'ta')
The draws below stay inside these ranges and needn't reach their ends.
Inputs may be any that keep to these rules, and one draw needn't show every extreme that they name: `lifetime`: positive. `keep`: positive.
All inputs are finite; a program needn't handle non-finite values. No bound on the sum of `tile_mask` on one device may be relied on, other than what follows from the above.
Results may differ from the reference program's by a relative error of at most 0.0003.
Values sent between devices are 32-bit elements; how exact they have to be, the bound alone decides.
No kernel may reach another device: no remote copies, remote signals or barrier semaphores. Data moves between devices by JAX's collectives and lax.ppermute only.
A program may use at most 128 MiB of HBM per device.

```python
import jax
import jax.numpy as jnp
from jax import lax

FIELD = 512
RADIUS = 8
PASSES = 7
SECTIONS = 96


def draw_lifetime(key, part):
    unit = jax.random.uniform(key, (FIELD, FIELD), jnp.float32)
    low_end, high_end = (0.5, 40.0)
    return jnp.exp(jnp.log(low_end) + unit * (jnp.log(high_end) - jnp.log(low_end)))


def draw_keep(key, part):
    base_key, spot_key, depth_random_key = jax.random.split(jax.random.fold_in(key, 11), 3)
    baseline_level = jax.random.uniform(base_key, (SECTIONS,), jnp.float32, 0.995, 1.0)
    bright_spots = jax.random.randint(spot_key, (4,), 0, SECTIONS)
    sudden_jump = jax.random.uniform(depth_random_key, (4,), jnp.float32, 0.5, 0.8)
    return baseline_level.at[bright_spots].set(sudden_jump)


def draw_coverage(key, part):
    heavy_key, light_key = jax.random.split(jax.random.fold_in(key, 23), 2)
    heavy_pick = jax.random.randint(heavy_key, (SECTIONS, FIELD, FIELD), 0, 48) == 0
    light_count = jax.random.randint(light_key, (SECTIONS, FIELD, FIELD), 0, 9)
    return jnp.where(heavy_pick, 4096, light_count).astype(jnp.int32)


def draw_log_mean(key, part):
    angle_key, slope_key, noise_key = jax.random.split(jax.random.fold_in(key, 31), 3)
    row_place = jnp.arange(FIELD).astype(jnp.float32) / (FIELD - 1) * 2.0 - 1.0
    col_place = jnp.arange(FIELD).astype(jnp.float32) / (FIELD - 1) * 2.0 - 1.0
    angle = jax.random.uniform(angle_key, (SECTIONS, 1, 1), jnp.float32, -3.14159, 3.14159)
    slope = jax.random.uniform(slope_key, (SECTIONS, 1, 1), jnp.float32, 2.5, 3.5)
    noise = jax.random.normal(noise_key, (SECTIONS, FIELD, FIELD), jnp.float32)
    ramp = slope * (jnp.cos(angle) * row_place[None, :, None] + jnp.sin(angle) * col_place[None, None, :])
    return jnp.clip(ramp + noise, -6.0, 6.0)


def touch_ends(entries, key, least, top_value):
    extent = entries.shape
    index_at = [jax.random.randint(jax.random.fold_in(key, axis), (), 0, extent[axis]) for axis in range(len(extent))]
    entries = entries.at[tuple(index_at)].set(least)
    longest = extent.index(max(extent))
    index_at[longest] = (index_at[longest] + 1) % extent[longest]
    return entries.at[tuple(index_at)].set(top_value)


def setup_inputs(seed: int = 0) -> dict:
    streams_of = jax.random.split(jax.random.key(seed), 6)
    return {
        "log_mean": draw_log_mean(jax.random.fold_in(streams_of[5], 71), 0),
        "tile_mask": touch_ends((jax.random.randint(streams_of[1], (SECTIONS, FIELD, FIELD), 0, 8) < 7).astype(jnp.int32), jax.random.fold_in(streams_of[1], 1), 0, 1),
        "coverage": draw_coverage(jax.random.fold_in(streams_of[5], 71), 0),
        "lifetime": draw_lifetime(jax.random.fold_in(streams_of[5], 71), 0),
        "keep": draw_keep(jax.random.fold_in(streams_of[5], 71), 0),
    }


def box_columns(values, radius):
    width_count = values.shape[-1]
    padded = jnp.pad(values, ((0, 0), (radius, radius)))
    running = padded[:, 0:width_count]
    for offset in range(1, 2 * radius + 1):
        running = running + padded[:, offset:offset + width_count]
    return running


def box_rowwise(values, radius):
    row_count = values.shape[0]
    padded = jnp.pad(values, ((radius, radius), (0, 0)))
    running = padded[0:row_count, :]
    for offset in range(1, 2 * radius + 1):
        running = running + padded[offset:offset + row_count, :]
    return running


def smooth_section(items):
    log_field, mask_field, count_field = items
    weight = 1.0 + mask_field.astype(jnp.float32) * count_field.astype(jnp.float32)
    denom = box_rowwise(box_columns(weight, RADIUS), RADIUS)
    field_now = log_field
    for level in range(PASSES):
        field_now = box_rowwise(box_columns(weight * field_now, RADIUS), RADIUS) / denom
    return field_now


def reference(log_mean, tile_mask, coverage, lifetime, keep):
    smoothed_field = lax.map(smooth_section, (log_mean, tile_mask, coverage))
    fade = jnp.exp(-lifetime / SECTIONS)
    zero_field = jnp.zeros((FIELD, FIELD), jnp.float32)

    def forward_turn(carry, items):
        mass, norm_sum = carry
        smooth_now, keep_now = items
        decay = keep_now * fade
        gain = 1.0 - decay
        mass = decay * mass + gain * smooth_now
        norm_sum = decay * norm_sum + gain
        return (mass, norm_sum), mass / norm_sum

    carry_end, forward_mean = lax.scan(forward_turn, (zero_field, zero_field), (smoothed_field, keep))

    def backward_turn(carry, items):
        mass, norm_sum = carry
        mean_now, keep_now, log_now, smooth_now = items
        decay = keep_now * fade
        gain = 1.0 - decay
        mass = decay * mass + gain * mean_now
        norm_sum = decay * norm_sum + gain
        return (mass, norm_sum), log_now - smooth_now + mass / norm_sum

    carry_back, corrected = lax.scan(backward_turn, (zero_field, zero_field), (forward_mean, keep, log_mean, smoothed_field), reverse=True)
    return corrected
```

```python
import jax
import jax.numpy as jnp
from jax import lax
from jax.experimental import pallas as pl
from jax.experimental.pallas import tpu as pltpu
from jax.sharding import PartitionSpec as P

RADIUS = 8
PASSES = 7
HALO = RADIUS * PASSES
LANES = 128
F32 = jnp.float32
BF16 = jnp.bfloat16
VM = pl.BlockSpec(memory_space=pltpu.VMEM)
SM = pl.BlockSpec(memory_space=pltpu.SMEM)


def edges_body(log_ref, mask_ref, cov_ref, first_ref, last_ref):
    rows = log_ref.shape[0]
    weight = 1.0 + mask_ref[...].astype(F32) * cov_ref[...].astype(F32)
    first_ref[0] = weight[:HALO]
    first_ref[1] = log_ref[:HALO]
    last_ref[0] = weight[rows - HALO:]
    last_ref[1] = log_ref[rows - HALO:]


def halves(values):
    high = values.astype(BF16)
    return high, (values - high.astype(F32)).astype(BF16)


def box(values, col_band, row_band):
    high, low = halves(values)
    cols = jnp.dot(high, col_band, preferred_element_type=F32) + jnp.dot(
        low, col_band, preferred_element_type=F32
    )
    rows_in = values.shape[0]
    rows_out = rows_in - 2 * RADIUS
    band = row_band[:rows_out, :rows_in]
    high, low = halves(cols)
    return jnp.dot(band, high, preferred_element_type=F32) + jnp.dot(
        band, low, preferred_element_type=F32
    )


def to_tiles(out_ref, values):
    rows, cols = values.shape
    place = 0
    for r in range(0, rows, 8):
        for c in range(0, cols, LANES):
            out_ref[place:place + 8, :] = values[r:r + 8, c:c + LANES]
            place += 8
    if place < out_ref.shape[0]:
        out_ref[place:, :] = jnp.zeros((out_ref.shape[0] - place, LANES), F32)


def smooth_body(log_ref, mask_ref, cov_ref, above_ref, below_ref, cb_ref, rb_ref, s_ref, e_ref):
    rows = log_ref.shape[0]
    own = 1.0 + mask_ref[...].astype(F32) * cov_ref[...].astype(F32)
    weight = jnp.concatenate([above_ref[0], own, below_ref[0]], axis=0)
    field = jnp.concatenate([above_ref[1], log_ref[...], below_ref[1]], axis=0)
    col_band = cb_ref[...]
    row_band = rb_ref[...]
    denom = jnp.maximum(box(weight, col_band, row_band), 1.0)
    inverse = 1.0 / denom
    total = rows + 2 * HALO
    scale = weight[RADIUS:total - RADIUS] * inverse
    now = weight * field
    trim = 0
    for level in range(PASSES):
        now = box(now, col_band, row_band)
        if level < PASSES - 1:
            now = now * scale[trim:scale.shape[0] - trim]
            trim += RADIUS
    smoothed = now * inverse[trim:inverse.shape[0] - trim]
    to_tiles(s_ref, smoothed)
    to_tiles(e_ref, log_ref[...] - smoothed)


def norms_body(keep_ref, fade_ref, fore_ref, back_ref):
    sections = keep_ref.shape[0]
    wide = fade_ref.shape[0]
    fade = fade_ref[...]
    norm = jnp.zeros_like(fade)
    for z in range(sections):
        decay = keep_ref[z] * fade
        gain = 1.0 - decay
        norm = decay * norm + gain
        fore_ref[z * wide:(z + 1) * wide, :] = gain / norm
    norm = jnp.zeros_like(fade)
    for z in reversed(range(sections)):
        decay = keep_ref[z] * fade
        norm = decay * norm + (1.0 - decay)
        back_ref[z * wide:(z + 1) * wide, :] = 1.0 / norm


def scan_body(keep_ref, fade_ref, fore_ref, back_ref, s_ref, out_ref):
    sections = keep_ref.shape[0]
    wide = fade_ref.shape[0]
    fade = fade_ref[...]
    mass = jnp.zeros_like(fade)
    for z in range(sections):
        decay = keep_ref[z] * fade
        at = slice(z * wide, (z + 1) * wide)
        mass = decay * mass + (1.0 - decay) * s_ref[at, :]
        out_ref[at, :] = mass * fore_ref[at, :]
    mass = jnp.zeros_like(fade)
    for z in reversed(range(sections)):
        decay = keep_ref[z] * fade
        at = slice(z * wide, (z + 1) * wide)
        mass = decay * mass + out_ref[at, :]
        out_ref[at, :] = mass * back_ref[at, :]


def pack_body(e_ref, drift_ref, out_ref):
    half = LANES // 2
    tiles = e_ref.shape[0] // 8
    across = out_ref.shape[0] * LANES // (tiles * 8 * LANES)
    del across
    blocks = out_ref.shape[0]
    per_row = blocks // 2
    row_tiles = tiles // per_row
    for c in range(per_row):
        for r in range(row_tiles // 2):
            top = (r * per_row + c) * 8
            low = ((r + row_tiles // 2) * per_row + c) * 8
            a = e_ref[top:top + 8, :] + drift_ref[top:top + 8, :]
            b = e_ref[low:low + 8, :] + drift_ref[low:low + 8, :]
            lane = lax.broadcasted_iota(jnp.int32, a.shape, 1) < half
            out_ref[2 * c, r * 8:(r + 1) * 8, :] = jnp.where(lane, a, pltpu.roll(b, half, 1))
            out_ref[2 * c + 1, r * 8:(r + 1) * 8, :] = jnp.where(lane, pltpu.roll(a, half, 1), b)


def unpack_body(in_ref, out_ref):
    half = LANES // 2
    blocks, depth, _ = in_ref.shape
    for t in range(blocks):
        values = in_ref[t]
        start = 2 * depth * t
        out_ref[start:start + depth, :] = values[:, :half]
        out_ref[start + depth:start + 2 * depth, :] = values[:, half:]


def shards(log_mean, tile_mask, coverage, lifetime, keep):
    rows, cols = log_mean.shape[1:]
    sections = keep.shape[0]
    size = lax.axis_size("ta")
    log2, mask2, cov2 = log_mean[0], tile_mask[0], coverage[0]
    edge = jax.ShapeDtypeStruct((2, HALO, cols), F32)
    first, last = pl.pallas_call(
        edges_body, out_shape=(edge, edge), in_specs=[VM] * 3, out_specs=(VM, VM), name="edges"
    )(log2, mask2, cov2)
    up = [(i, i + 1) for i in range(size - 1)]
    down = [(j, i) for i, j in up]
    above = lax.ppermute(last, "ta", up)
    below = lax.ppermute(first, "ta", down)

    used = rows * cols // LANES
    wide = -(-used // sections)
    padded = sections * wide
    tiled = lifetime.reshape(rows // 8, 8, cols // LANES, LANES).transpose(0, 2, 1, 3)
    tiled = jnp.pad(tiled.reshape(used, LANES), ((0, padded - used), (0, 0)), constant_values=1.0)
    mine = lax.dynamic_slice_in_dim(tiled, lax.axis_index("gz") * wide, wide)
    fade = jnp.exp(-mine / sections)
    long = jax.ShapeDtypeStruct((padded, LANES), F32)
    fore, back = pl.pallas_call(
        norms_body, out_shape=(long, long), in_specs=[SM, VM], out_specs=(VM, VM), name="norms"
    )(keep, fade)

    place = jnp.arange(cols)
    col_band = (jnp.abs(place[:, None] - place[None, :]) <= RADIUS).astype(BF16)
    total = rows + 2 * HALO
    offset = jnp.arange(total)[None, :] - jnp.arange(total - 2 * RADIUS)[:, None]
    row_band = ((offset >= 0) & (offset <= 2 * RADIUS)).astype(BF16)
    smoothed, rest = pl.pallas_call(
        smooth_body,
        out_shape=(long, jax.ShapeDtypeStruct((used, LANES), F32)),
        in_specs=[VM] * 7,
        out_specs=(VM, VM),
        name="smooth",
    )(log2, mask2, cov2, above, below, col_band, row_band)

    def swap(values):
        flat = values.reshape(padded * LANES)
        flat = lax.all_to_all(flat, "gz", 0, 0, tiled=True)
        return flat.reshape(padded, LANES)

    drift = pl.pallas_call(
        scan_body, out_shape=long, in_specs=[SM] + [VM] * 4, out_specs=VM, name="scan"
    )(keep, fade, fore, back, swap(smoothed))
    drift = swap(drift)
    packed = pl.pallas_call(
        pack_body,
        out_shape=jax.ShapeDtypeStruct((size, used // size, LANES), F32),
        in_specs=[VM] * 2,
        out_specs=VM,
        name="pack",
    )(rest, drift)
    packed = lax.all_to_all(packed, "ta", 0, 0, tiled=True)
    out = pl.pallas_call(
        unpack_body,
        out_shape=jax.ShapeDtypeStruct((size * rows, cols // size), F32),
        in_specs=[VM],
        out_specs=VM,
        name="unpack",
    )(packed)
    return out[None]


def solution(mesh):
    return jax.shard_map(
        shards,
        mesh=mesh,
        in_specs=(
            P("gz", "ta", None),
            P("gz", "ta", None),
            P("gz", "ta", None),
            P("ta", None),
            P(),
        ),
        out_specs=P("gz", None, "ta"),
        check_vma=False,
    )
```

```python
import jax
import jax.numpy as jnp
from jax import lax
from jax.experimental import pallas as pl
from jax.experimental.pallas import tpu as pltpu
from jax.sharding import PartitionSpec as P

RADIUS = 8
PASSES = 7
HALO = RADIUS * PASSES
LANES = 128
F32 = jnp.float32
BF16 = jnp.bfloat16
VM = pl.BlockSpec(memory_space=pltpu.VMEM)
SM = pl.BlockSpec(memory_space=pltpu.SMEM)


def edges_body(log_ref, mask_ref, cov_ref, first_ref, last_ref):
    rows = log_ref.shape[0]
    weight = 1.0 + mask_ref[...].astype(F32) * cov_ref[...].astype(F32)
    first_ref[0] = weight[:HALO]
    first_ref[1] = log_ref[:HALO]
    last_ref[0] = weight[rows - HALO:]
    last_ref[1] = log_ref[rows - HALO:]


def halves(values):
    high = values.astype(BF16)
    return high, (values - high.astype(F32)).astype(BF16)


def box(values, col_band, row_band):
    high, low = halves(values)
    cols = jnp.dot(high, col_band, preferred_element_type=F32) + jnp.dot(
        low, col_band, preferred_element_type=F32
    )
    rows_in = values.shape[0]
    rows_out = rows_in - 2 * RADIUS
    band = row_band[:rows_out, :rows_in]
    high, low = halves(cols)
    return jnp.dot(band, high, preferred_element_type=F32) + jnp.dot(
        band, low, preferred_element_type=F32
    )


def to_tiles(out_ref, values):
    rows, cols = values.shape
    place = 0
    for r in range(0, rows, 8):
        for c in range(0, cols, LANES):
            out_ref[place:place + 8, :] = values[r:r + 8, c:c + LANES]
            place += 8
    if place < out_ref.shape[0]:
        out_ref[place:, :] = jnp.zeros((out_ref.shape[0] - place, LANES), F32)


def smooth_body(log_ref, mask_ref, cov_ref, above_ref, below_ref, cb_ref, rb_ref, s_ref, e_ref):
    rows = log_ref.shape[0]
    own = 1.0 + mask_ref[...].astype(F32) * cov_ref[...].astype(F32)
    weight = jnp.concatenate([above_ref[0], own, below_ref[0]], axis=0)
    field = jnp.concatenate([above_ref[1], log_ref[...], below_ref[1]], axis=0)
    col_band = cb_ref[...]
    row_band = rb_ref[...]
    denom = jnp.maximum(box(weight, col_band, row_band), 1.0)
    inverse = 1.0 / denom
    total = rows + 2 * HALO
    scale = weight[RADIUS:total - RADIUS] * inverse
    now = weight * field
    trim = 0
    for level in range(PASSES):
        now = box(now, col_band, row_band)
        if level < PASSES - 1:
            now = now * scale[trim:scale.shape[0] - trim]
            trim += RADIUS
    smoothed = now * inverse[trim:inverse.shape[0] - trim]
    to_tiles(s_ref, smoothed)
    to_tiles(e_ref, log_ref[...] - smoothed)


def norms_body(keep_ref, fade_ref, fore_ref, back_ref):
    sections = keep_ref.shape[0]
    wide = fade_ref.shape[0]
    fade = fade_ref[...]
    norm = jnp.zeros_like(fade)
    for z in range(sections):
        decay = keep_ref[z] * fade
        gain = 1.0 - decay
        norm = decay * norm + gain
        fore_ref[z * wide:(z + 1) * wide, :] = gain / norm
    norm = jnp.zeros_like(fade)
    for z in reversed(range(sections)):
        decay = keep_ref[z] * fade
        norm = decay * norm + (1.0 - decay)
        back_ref[z * wide:(z + 1) * wide, :] = 1.0 / norm


def scan_body(keep_ref, fade_ref, fore_ref, back_ref, s_ref, out_ref):
    sections = keep_ref.shape[0]
    wide = fade_ref.shape[0]
    fade = fade_ref[...]
    mass = jnp.zeros_like(fade)
    for z in range(sections):
        decay = keep_ref[z] * fade
        at = slice(z * wide, (z + 1) * wide)
        mass = decay * mass + (1.0 - decay) * s_ref[at, :]
        out_ref[at, :] = mass * fore_ref[at, :]
    mass = jnp.zeros_like(fade)
    for z in reversed(range(sections)):
        decay = keep_ref[z] * fade
        at = slice(z * wide, (z + 1) * wide)
        mass = decay * mass + out_ref[at, :]
        out_ref[at, :] = mass * back_ref[at, :]


def pack_body(e_ref, drift_ref, out_ref):
    half = LANES // 2
    tiles = e_ref.shape[0] // 8
    across = out_ref.shape[0] * LANES // (tiles * 8 * LANES)
    del across
    blocks = out_ref.shape[0]
    per_row = blocks // 2
    row_tiles = tiles // per_row
    for c in range(per_row):
        for r in range(row_tiles // 2):
            top = (r * per_row + c) * 8
            low = ((r + row_tiles // 2) * per_row + c) * 8
            a = e_ref[top:top + 8, :] + drift_ref[top:top + 8, :]
            b = e_ref[low:low + 8, :] + drift_ref[low:low + 8, :]
            lane = lax.broadcasted_iota(jnp.int32, a.shape, 1) < half
            out_ref[2 * c, r * 8:(r + 1) * 8, :] = jnp.where(lane, a, pltpu.roll(b, half, 1))
            out_ref[2 * c + 1, r * 8:(r + 1) * 8, :] = jnp.where(lane, pltpu.roll(a, half, 1), b)


def unpack_body(in_ref, out_ref):
    half = LANES // 2
    blocks, depth, _ = in_ref.shape
    for t in range(blocks):
        values = in_ref[t]
        start = 2 * depth * t
        out_ref[start:start + depth, :] = values[:, :half]
        out_ref[start + depth:start + 2 * depth, :] = values[:, half:]


def shards(log_mean, tile_mask, coverage, lifetime, keep):
    rows, cols = log_mean.shape[1:]
    sections = keep.shape[0]
    size = lax.axis_size("ta")
    log2, mask2, cov2 = log_mean[0], tile_mask[0], coverage[0]
    edge = jax.ShapeDtypeStruct((2, HALO, cols), F32)
    first, last = pl.pallas_call(
        edges_body, out_shape=(edge, edge), in_specs=[VM] * 3, out_specs=(VM, VM), name="edges", compiler_params=pltpu.CompilerParams(vmem_limit_bytes=16<<20)
    )(log2, mask2, cov2)
    up = [(i, i + 1) for i in range(size - 1)]
    down = [(j, i) for i, j in up]
    above = lax.ppermute(last, "ta", up)
    below = lax.ppermute(first, "ta", down)

    used = rows * cols // LANES
    wide = -(-used // sections)
    padded = sections * wide
    tiled = lifetime.reshape(rows // 8, 8, cols // LANES, LANES).transpose(0, 2, 1, 3)
    tiled = jnp.pad(tiled.reshape(used, LANES), ((0, padded - used), (0, 0)), constant_values=1.0)
    mine = lax.dynamic_slice_in_dim(tiled, lax.axis_index("gz") * wide, wide)
    fade = jnp.exp(-mine / sections)
    long = jax.ShapeDtypeStruct((padded, LANES), F32)
    fore, back = pl.pallas_call(
        norms_body, out_shape=(long, long), in_specs=[SM, VM], out_specs=(VM, VM), name="norms", compiler_params=pltpu.CompilerParams(vmem_limit_bytes=16<<20)
    )(keep, fade)

    place = jnp.arange(cols)
    col_band = (jnp.abs(place[:, None] - place[None, :]) <= RADIUS).astype(BF16)
    total = rows + 2 * HALO
    offset = jnp.arange(total)[None, :] - jnp.arange(total - 2 * RADIUS)[:, None]
    row_band = ((offset >= 0) & (offset <= 2 * RADIUS)).astype(BF16)
    smoothed, rest = pl.pallas_call(
        smooth_body,
        out_shape=(long, jax.ShapeDtypeStruct((used, LANES), F32)),
        in_specs=[VM] * 7,
        out_specs=(VM, VM),
        name="smooth", compiler_params=pltpu.CompilerParams(vmem_limit_bytes=16<<20),
    )(log2, mask2, cov2, above, below, col_band, row_band)

    def swap(values):
        flat = values.reshape(padded * LANES)
        flat = lax.all_to_all(flat, "gz", 0, 0, tiled=True)
        return flat.reshape(padded, LANES)

    drift = pl.pallas_call(
        scan_body, out_shape=long, in_specs=[SM] + [VM] * 4, out_specs=VM, name="scan", compiler_params=pltpu.CompilerParams(vmem_limit_bytes=16<<20)
    )(keep, fade, fore, back, swap(smoothed))
    drift = swap(drift)
    packed = pl.pallas_call(
        pack_body,
        out_shape=jax.ShapeDtypeStruct((size, used // size, LANES), F32),
        in_specs=[VM] * 2,
        out_specs=VM,
        name="pack", compiler_params=pltpu.CompilerParams(vmem_limit_bytes=16<<20),
    )(rest, drift)
    packed = lax.all_to_all(packed, "ta", 0, 0, tiled=True)
    out = pl.pallas_call(
        unpack_body,
        out_shape=jax.ShapeDtypeStruct((size * rows, cols // size), F32),
        in_specs=[VM],
        out_specs=VM,
        name="unpack", compiler_params=pltpu.CompilerParams(vmem_limit_bytes=16<<20),
    )(packed)
    return out[None]


def solution(mesh):
    return jax.shard_map(
        shards,
        mesh=mesh,
        in_specs=(
            P("gz", "ta", None),
            P("gz", "ta", None),
            P("gz", "ta", None),
            P("ta", None),
            P(),
        ),
        out_specs=P("gz", None, "ta"),
        check_vma=False,
    )
```

```python
import jax
import jax.numpy as jnp
import numpy as np
from jax import lax
from jax.experimental import pallas as pl
from jax.experimental.pallas import tpu as pltpu
from jax.sharding import PartitionSpec as P

RADIUS = 8
PASSES = 7
HALO = RADIUS * PASSES
LANES = 128
F32 = jnp.float32
BF16 = jnp.bfloat16
VM = pl.BlockSpec(memory_space=pltpu.VMEM)
SM = pl.BlockSpec(memory_space=pltpu.SMEM)
PARAMS = pltpu.CompilerParams(vmem_limit_bytes=16 << 20)


def prepare_body(wide, log_ref, mask_ref, cov_ref, life_ref, out_ref, both_ref, life_t_ref):
    rows, cols = log_ref.shape
    parts, depth, _ = out_ref.shape
    share = cols // parts
    span = share + 2 * HALO
    weight = 1.0 + mask_ref[...].astype(F32) * cov_ref[...].astype(F32)
    both = jnp.concatenate([weight, log_ref[...]], axis=0)
    life = jnp.concatenate([life_ref[...], life_ref[...]], axis=0)
    both_ref[:HALO, :] = jnp.zeros((HALO, LANES), F32)
    both_ref[HALO + cols:, :] = jnp.zeros((HALO, LANES), F32)
    for c in range(0, cols, LANES):
        both_ref[HALO + c:HALO + c + LANES, :] = both[:, c:c + LANES].T
        life_t_ref[c:c + LANES, :] = life[:, c:c + LANES].T
    first = lax.axis_index("gz") * wide
    for t in range(parts):
        out_ref[t, :span, :] = both_ref[share * t:share * t + span, :]
        out_ref[t, span:, :] = jnp.zeros((depth - span, LANES), F32)
        for i in range(wide):
            place = share * t + (first + i) % share
            out_ref[t, span + i:span + i + 1, :] = life_t_ref[pl.ds(place, 1), :]


def halves(values):
    high = values.astype(BF16)
    return high, (values - high.astype(F32)).astype(BF16)


def box(values, col_band, row_band):
    high, low = halves(values)
    cols = jnp.dot(high, col_band, preferred_element_type=F32) + jnp.dot(
        low, col_band, preferred_element_type=F32
    )
    rows_in = values.shape[0]
    rows_out = rows_in - 2 * RADIUS
    band = row_band[:rows_out, :rows_in]
    high, low = halves(cols)
    return jnp.dot(band, high, preferred_element_type=F32) + jnp.dot(
        band, low, preferred_element_type=F32
    )


def smooth_body(wide, in_ref, cb_ref, rb_ref, s_ref, e_ref, life_ref):
    parts = in_ref.shape[0]
    half = LANES // 2
    total = rb_ref.shape[1]
    share = total - 2 * HALO
    left = lax.broadcasted_iota(jnp.int32, (total, LANES), 1) < half
    weights, fields = [], []
    for t in range(0, parts, 2):
        a = in_ref[t, :total, :]
        b = in_ref[t + 1, :total, :]
        weights.append(jnp.where(left, a, pltpu.roll(b, half, 1)))
        fields.append(jnp.where(left, pltpu.roll(a, half, 1), b))
    weight = jnp.concatenate(weights, axis=1)
    field = jnp.concatenate(fields, axis=1)

    first = lax.axis_index("gz") * wide
    left = lax.broadcasted_iota(jnp.int32, (1, LANES), 1) < half
    for i in range(wide):
        pair = 2 * jnp.minimum((first + i) // share, parts // 2 - 1)
        a = in_ref[pair, total + i:total + i + 1, :]
        b = in_ref[pair + 1, total + i:total + i + 1, :]
        life_ref[i:i + 1, :] = jnp.where(left, a, b)

    col_band = cb_ref[...]
    row_band = rb_ref[...]
    denom = jnp.maximum(box(weight, col_band, row_band), 1.0)
    inverse = 1.0 / denom
    scale = weight[RADIUS:total - RADIUS] * inverse
    now = weight * field
    trim = 0
    for level in range(PASSES):
        now = box(now, col_band, row_band)
        if level < PASSES - 1:
            now = now * scale[trim:scale.shape[0] - trim]
            trim += RADIUS
    smoothed = now * inverse[trim:inverse.shape[0] - trim]
    rest = field[HALO:HALO + share] - smoothed
    for c in range(parts // 2):
        s_ref[c * share:(c + 1) * share, :] = smoothed[:, c * LANES:(c + 1) * LANES]
        e_ref[c * share:(c + 1) * share, :] = rest[:, c * LANES:(c + 1) * LANES]
    used = e_ref.shape[0]
    s_ref[used:, :] = jnp.zeros((s_ref.shape[0] - used, LANES), F32)


def norms_body(keep_ref, life_ref, fade_ref, fore_ref, back_ref):
    sections = keep_ref.shape[0]
    wide = life_ref.shape[0]
    fade = jnp.exp(-life_ref[...] / sections)
    fade_ref[...] = fade
    norm = jnp.zeros_like(fade)
    for z in range(sections):
        decay = keep_ref[z] * fade
        gain = 1.0 - decay
        norm = decay * norm + gain
        fore_ref[z * wide:(z + 1) * wide, :] = gain / norm
    norm = jnp.zeros_like(fade)
    for z in reversed(range(sections)):
        decay = keep_ref[z] * fade
        norm = decay * norm + (1.0 - decay)
        back_ref[z * wide:(z + 1) * wide, :] = 1.0 / norm


def scan_body(keep_ref, fade_ref, fore_ref, back_ref, s_ref, out_ref):
    sections = keep_ref.shape[0]
    wide = fade_ref.shape[0]
    fade = fade_ref[...]
    mass = jnp.zeros_like(fade)
    for z in range(sections):
        decay = keep_ref[z] * fade
        at = slice(z * wide, (z + 1) * wide)
        mass = decay * mass + (1.0 - decay) * s_ref[at, :]
        out_ref[at, :] = mass * fore_ref[at, :]
    mass = jnp.zeros_like(fade)
    for z in reversed(range(sections)):
        decay = keep_ref[z] * fade
        at = slice(z * wide, (z + 1) * wide)
        mass = decay * mass + out_ref[at, :]
        out_ref[at, :] = mass * back_ref[at, :]


def finish_body(e_ref, drift_ref, out_ref):
    share = out_ref.shape[0]
    for c in range(out_ref.shape[1] // LANES):
        at = slice(c * share, (c + 1) * share)
        out_ref[:, c * LANES:(c + 1) * LANES] = e_ref[at, :] + drift_ref[at, :]


def call(body, name, outs, ins, scratch=()):
    return pl.pallas_call(
        body,
        out_shape=outs,
        in_specs=ins,
        out_specs=jax.tree.map(lambda _: VM, outs),
        scratch_shapes=scratch,
        compiler_params=PARAMS,
        name=name,
    )


def shape(*dims):
    return jax.ShapeDtypeStruct(dims, F32)


def shards(log_mean, tile_mask, coverage, lifetime, keep):
    rows, cols = log_mean.shape[1:]
    sections = keep.shape[0]
    parts = lax.axis_size("ta")
    share = cols // parts
    total = share + 2 * HALO
    used = rows * cols // LANES
    wide = -(-used // sections)
    padded = sections * wide

    sent = call(
        lambda *refs: prepare_body(wide, *refs),
        "prepare",
        shape(parts, total + 8, LANES),
        [VM] * 4,
        (pltpu.VMEM((cols + 2 * HALO, LANES), F32), pltpu.VMEM((cols, LANES), F32)),
    )(log_mean[0], tile_mask[0], coverage[0], lifetime)
    sent = lax.all_to_all(sent, "ta", 0, 0, tiled=True)

    place = np.arange(rows * parts)
    col_band = (np.abs(place[:, None] - place[None, :]) <= RADIUS).astype(BF16)
    offset = np.arange(total)[None, :] - np.arange(total - 2 * RADIUS)[:, None]
    row_band = ((offset >= 0) & (offset <= 2 * RADIUS)).astype(BF16)
    smoothed, rest, life = call(
        lambda *refs: smooth_body(wide, *refs),
        "smooth",
        (shape(padded, LANES), shape(used, LANES), shape(wide, LANES)),
        [VM] * 3,
    )(sent, col_band, row_band)

    def swap(values):
        flat = values.reshape(padded * LANES)
        flat = lax.all_to_all(flat, "gz", 0, 0, tiled=True)
        return flat.reshape(padded, LANES)

    long = shape(padded, LANES)
    fade, fore, back = call(
        norms_body, "norms", (shape(wide, LANES), long, long), [SM, VM]
    )(keep, life)
    drift = call(scan_body, "scan", long, [SM] + [VM] * 4)(
        keep, fade, fore, back, swap(smoothed)
    )
    out = call(finish_body, "finish", shape(share, rows * parts), [VM] * 2)(rest, swap(drift))
    return out.T[None]


def solution(mesh):
    return jax.shard_map(
        shards,
        mesh=mesh,
        in_specs=(
            P("gz", "ta", None),
            P("gz", "ta", None),
            P("gz", "ta", None),
            P("ta", None),
            P(),
        ),
        out_specs=P("gz", None, "ta"),
        check_vma=False,
    )
```

```python
import jax
import jax.numpy as jnp
import numpy as np
from jax import lax
from jax.experimental import pallas as pl
from jax.experimental.pallas import tpu as pltpu
from jax.sharding import PartitionSpec as P

RADIUS = 8
PASSES = 7
HALO = RADIUS * PASSES
LANES = 128
F32 = jnp.float32
BF16 = jnp.bfloat16
VM = pl.BlockSpec(memory_space=pltpu.VMEM)
HB = pl.BlockSpec(memory_space=pltpu.HBM)
SM = pl.BlockSpec(memory_space=pltpu.SMEM)
PARAMS = pltpu.CompilerParams(vmem_limit_bytes=16 << 20)


def prepare_body(
    wide, log_hbm, mask_hbm, cov_hbm, life_hbm, out_ref,
    log_ref, mask_ref, cov_ref, life_ref, both_ref, life_t_ref, sems,
):
    pairs = ((life_hbm, life_ref), (log_hbm, log_ref), (mask_hbm, mask_ref), (cov_hbm, cov_ref))
    copies = [pltpu.make_async_copy(a, b, sems.at[i]) for i, (a, b) in enumerate(pairs)]
    for copy in copies:
        copy.start()
    rows, cols = log_ref.shape
    parts, depth, _ = out_ref.shape
    share = cols // parts
    span = share + 2 * HALO
    both_ref[:HALO, :] = jnp.zeros((HALO, LANES), F32)
    both_ref[HALO + cols:, :] = jnp.zeros((HALO, LANES), F32)
    copies[0].wait()
    life = jnp.concatenate([life_ref[...], life_ref[...]], axis=0)
    for c in range(0, cols, LANES):
        life_t_ref[c:c + LANES, :] = life[:, c:c + LANES].T
    for copy in copies[1:]:
        copy.wait()
    weight = 1.0 + mask_ref[...].astype(F32) * cov_ref[...].astype(F32)
    both = jnp.concatenate([weight, log_ref[...]], axis=0)
    for c in range(0, cols, LANES):
        both_ref[HALO + c:HALO + c + LANES, :] = both[:, c:c + LANES].T
    first = lax.axis_index("gz") * wide
    for t in range(parts):
        out_ref[t, :span, :] = both_ref[share * t:share * t + span, :]
        out_ref[t, span:, :] = jnp.zeros((depth - span, LANES), F32)
        for i in range(wide):
            place = share * t + (first + i) % share
            out_ref[t, span + i:span + i + 1, :] = life_t_ref[pl.ds(place, 1), :]


def halves(values):
    high = values.astype(BF16)
    return high, (values - high.astype(F32)).astype(BF16)


def dot(a, b):
    return jnp.dot(a, b, preferred_element_type=F32)


def along_lanes(tiles, band, joint):
    values = jnp.concatenate(tiles, axis=0)
    rows = values.shape[0]
    half = band.shape[0]
    edge = half // 2
    both = jnp.concatenate(halves(values), axis=0)
    sides = dot(jnp.concatenate([both[:, :half], both[:, half:]], axis=0), band)
    left, right = sides[:2 * rows], sides[2 * rows:]
    across = dot(both[:, edge:half + edge], joint)
    both = jnp.concatenate(
        [
            left[:, :edge],
            left[:, edge:] + across[:, :edge],
            right[:, :edge] + across[:, edge:],
            right[:, edge:],
        ],
        axis=1,
    )
    sums = both[:rows] + both[rows:]
    return [sums[r:r + 8] for r in range(0, rows, 8)]


def along_rows(tiles):
    count = len(tiles)
    row = lax.broadcasted_iota(jnp.int32, tiles[0].shape, 0)
    level = tiles
    for k in (1, 2, 4):
        turned = [pltpu.roll(v, 8 - k, 0) for v in level]
        after = turned[1:] + turned[-1:]
        level = [
            v + jnp.where(row < 8 - k, a, b) for v, a, b in zip(level, turned, after)
        ]
    return [level[j] + level[j + 1] + tiles[j + 2] for j in range(count - 2)]


def box(tiles, band, joint):
    return along_rows(along_lanes(tiles, band, joint))


def smooth_body(
    wide, in_ref, band_ref, joint_ref, s_ref, e_ref, life_ref, inverse_ref, scale_ref
):
    parts = in_ref.shape[0]
    half = LANES // 2
    total = inverse_ref.shape[0] + 2 * RADIUS
    share = total - 2 * HALO
    left = lax.broadcasted_iota(jnp.int32, (total, LANES), 1) < half
    weights, fields = [], []
    for t in range(0, parts, 2):
        a = in_ref[t, :total, :]
        b = in_ref[t + 1, :total, :]
        weights.append(jnp.where(left, a, pltpu.roll(b, half, 1)))
        fields.append(jnp.where(left, pltpu.roll(a, half, 1), b))
    weight = jnp.concatenate(weights, axis=1)
    field = jnp.concatenate(fields, axis=1)

    first = lax.axis_index("gz") * wide
    left = lax.broadcasted_iota(jnp.int32, (1, LANES), 1) < half
    for i in range(wide):
        pair = 2 * jnp.minimum((first + i) // share, parts // 2 - 1)
        a = in_ref[pair, total + i:total + i + 1, :]
        b = in_ref[pair + 1, total + i:total + i + 1, :]
        life_ref[i:i + 1, :] = jnp.where(left, a, b)

    band = band_ref[...]
    joint = joint_ref[...]
    weights = [weight[r:r + 8] for r in range(0, total, 8)]
    now = [w * field[8 * j:8 * j + 8] for j, w in enumerate(weights)]
    denoms = box(weights, band, joint)
    inverse = [1.0 / jnp.maximum(d, 1.0) for d in denoms]
    for j, value in enumerate(inverse):
        inverse_ref[8 * j:8 * j + 8, :] = value
        scale_ref[8 * j:8 * j + 8, :] = value * weights[j + 1]
    for level in range(PASSES):
        now = box(now, band, joint)
        factor = scale_ref if level < PASSES - 1 else inverse_ref
        now = [
            v * factor[8 * (j + level):8 * (j + level + 1), :] for j, v in enumerate(now)
        ]
    smoothed = jnp.concatenate(now, axis=0)
    rest = field[HALO:HALO + share] - smoothed
    for c in range(parts // 2):
        s_ref[c * share:(c + 1) * share, :] = smoothed[:, c * LANES:(c + 1) * LANES]
        e_ref[c * share:(c + 1) * share, :] = rest[:, c * LANES:(c + 1) * LANES]
    used = e_ref.shape[0]
    s_ref[used:, :] = jnp.zeros((s_ref.shape[0] - used, LANES), F32)


def norms_body(keep_ref, life_ref, fade_ref, fore_ref, back_ref):
    sections = keep_ref.shape[0]
    wide = life_ref.shape[0]
    fade = jnp.exp(-life_ref[...] / sections)
    fade_ref[...] = fade
    norm = jnp.zeros_like(fade)
    for z in range(sections):
        decay = keep_ref[z] * fade
        gain = 1.0 - decay
        norm = decay * norm + gain
        fore_ref[z * wide:(z + 1) * wide, :] = gain / norm
    norm = jnp.zeros_like(fade)
    for z in reversed(range(sections)):
        decay = keep_ref[z] * fade
        norm = decay * norm + (1.0 - decay)
        back_ref[z * wide:(z + 1) * wide, :] = 1.0 / norm


def scan_body(keep_ref, fade_ref, fore_ref, back_ref, s_ref, out_ref):
    sections = keep_ref.shape[0]
    wide = fade_ref.shape[0]
    fade = fade_ref[...]
    mass = jnp.zeros_like(fade)
    for z in range(sections):
        decay = keep_ref[z] * fade
        at = slice(z * wide, (z + 1) * wide)
        mass = decay * mass + (1.0 - decay) * s_ref[at, :]
        out_ref[at, :] = mass * fore_ref[at, :]
    mass = jnp.zeros_like(fade)
    for z in reversed(range(sections)):
        decay = keep_ref[z] * fade
        at = slice(z * wide, (z + 1) * wide)
        mass = decay * mass + out_ref[at, :]
        out_ref[at, :] = mass * back_ref[at, :]


def finish_body(e_ref, drift_ref, out_ref):
    share = out_ref.shape[0]
    for c in range(out_ref.shape[1] // LANES):
        at = slice(c * share, (c + 1) * share)
        out_ref[:, c * LANES:(c + 1) * LANES] = e_ref[at, :] + drift_ref[at, :]


def call(body, name, outs, ins, scratch=()):
    return pl.pallas_call(
        body,
        out_shape=outs,
        in_specs=ins,
        out_specs=jax.tree.map(lambda _: VM, outs),
        scratch_shapes=scratch,
        compiler_params=PARAMS,
        name=name,
    )


def in_hbm(values):
    return pltpu.with_memory_space_constraint(values, pltpu.HBM)


def shape(*dims):
    return jax.ShapeDtypeStruct(dims, F32)


def shards(log_mean, tile_mask, coverage, lifetime, keep):
    rows, cols = log_mean.shape[1:]
    sections = keep.shape[0]
    parts = lax.axis_size("ta")
    share = cols // parts
    total = share + 2 * HALO
    used = rows * cols // LANES
    wide = -(-used // sections)
    padded = sections * wide

    sent = call(
        lambda *refs: prepare_body(wide, *refs),
        "prepare",
        shape(parts, total + 8, LANES),
        [HB] * 4,
        [pltpu.VMEM((rows, cols), a.dtype) for a in (log_mean, tile_mask, coverage, lifetime)]
        + [pltpu.VMEM((cols + 2 * HALO, LANES), F32), pltpu.VMEM((cols, LANES), F32)]
        + [pltpu.SemaphoreType.DMA((4,))],
    )(*(in_hbm(a) for a in (log_mean[0], tile_mask[0], coverage[0], lifetime)))
    sent = lax.all_to_all(sent, "ta", 0, 0, tiled=True)

    half = np.arange(rows * parts // 2)
    near = np.abs(half[:, None] - half[None, :]) <= RADIUS
    left = half < half.size // 2
    band = near.astype(BF16)
    joint = (near & (left[:, None] != left[None, :])).astype(BF16)
    smoothed, rest, life = call(
        lambda *refs: smooth_body(wide, *refs),
        "smooth",
        (shape(padded, LANES), shape(used, LANES), shape(wide, LANES)),
        [VM] * 3,
        [pltpu.VMEM((total - 2 * RADIUS, rows * parts), F32)] * 2,
    )(sent, band, joint)

    def swap(values):
        flat = values.reshape(padded * LANES)
        flat = lax.all_to_all(flat, "gz", 0, 0, tiled=True)
        return flat.reshape(padded, LANES)

    long = shape(padded, LANES)
    fade, fore, back = call(
        norms_body, "norms", (shape(wide, LANES), long, long), [SM, VM]
    )(keep, life)
    drift = call(scan_body, "scan", long, [SM] + [VM] * 4)(
        keep, fade, fore, back, swap(smoothed)
    )
    out = call(finish_body, "finish", shape(share, rows * parts), [VM] * 2)(rest, swap(drift))
    return out.T[None]


def solution(mesh):
    return jax.shard_map(
        shards,
        mesh=mesh,
        in_specs=(
            P("gz", "ta", None),
            P("gz", "ta", None),
            P("gz", "ta", None),
            P("ta", None),
            P(),
        ),
        out_specs=P("gz", None, "ta"),
        check_vma=False,
    )
```

```python
import jax
import jax.numpy as jnp
import numpy as np
from jax import lax
from jax.experimental import pallas as pl
from jax.experimental.pallas import tpu as pltpu
from jax.sharding import PartitionSpec as P

RADIUS = 8
PASSES = 7
HALO = RADIUS * PASSES
START = 67
LANES = 128
F32 = jnp.float32
BF16 = jnp.bfloat16
VM = pl.BlockSpec(memory_space=pltpu.VMEM)
HB = pl.BlockSpec(memory_space=pltpu.HBM)
SM = pl.BlockSpec(memory_space=pltpu.SMEM)
PARAMS = pltpu.CompilerParams(vmem_limit_bytes=16 << 20)


def prepare_body(
    wide, turn, log_hbm, mask_hbm, cov_hbm, life_hbm, out_ref,
    log_ref, mask_ref, cov_ref, life_ref, both_ref, life_t_ref, sems,
):
    pairs = ((life_hbm, life_ref), (log_hbm, log_ref), (mask_hbm, mask_ref), (cov_hbm, cov_ref))
    copies = [pltpu.make_async_copy(a, b, sems.at[i]) for i, (a, b) in enumerate(pairs)]
    for copy in copies:
        copy.start()
    rows, cols = log_ref.shape
    parts, depth, _ = out_ref.shape
    share = cols // parts
    span = share + 2 * HALO
    both_ref[:HALO, :] = jnp.zeros((HALO, LANES), F32)
    both_ref[HALO + cols:, :] = jnp.zeros((HALO, LANES), F32)
    copies[0].wait()
    life = jnp.concatenate([life_ref[...], life_ref[...]], axis=0)
    for c in range(0, cols, LANES):
        life_t_ref[c:c + LANES, :] = life[:, c:c + LANES].T
    for copy in copies[1:]:
        copy.wait()
    weight = 1.0 + mask_ref[...].astype(F32) * cov_ref[...].astype(F32)
    both = jnp.concatenate([weight, log_ref[...]], axis=0)
    for c in range(0, cols, LANES):
        both_ref[HALO + c:HALO + c + LANES, :] = both[:, c:c + LANES].T
    sections = lax.axis_size("gz")
    first = lax.rem(lax.axis_index("gz") + sections - turn, sections) * wide
    for t in range(parts):
        out_ref[t, :span, :] = both_ref[share * t:share * t + span, :]
        out_ref[t, span:, :] = jnp.zeros((depth - span, LANES), F32)
        for i in range(wide):
            place = share * t + (first + i) % share
            out_ref[t, span + i:span + i + 1, :] = life_t_ref[pl.ds(place, 1), :]


def halves(values):
    high = values.astype(BF16)
    return high, (values - high.astype(F32)).astype(BF16)


def dot(a, b):
    return jnp.dot(a, b, preferred_element_type=F32)


def along_lanes(tiles, band, joint):
    values = jnp.concatenate(tiles, axis=0)
    rows = values.shape[0]
    half = band.shape[0]
    edge = half // 2
    both = jnp.concatenate(halves(values), axis=0)
    sides = dot(jnp.concatenate([both[:, :half], both[:, half:]], axis=0), band)
    left, right = sides[:2 * rows], sides[2 * rows:]
    across = dot(both[:, edge:half + edge], joint)
    both = jnp.concatenate(
        [
            left[:, :edge],
            left[:, edge:] + across[:, :edge],
            right[:, :edge] + across[:, edge:],
            right[:, edge:],
        ],
        axis=1,
    )
    sums = both[:rows] + both[rows:]
    return [sums[r:r + 8] for r in range(0, rows, 8)]


def along_rows(tiles):
    count = len(tiles)
    row = lax.broadcasted_iota(jnp.int32, tiles[0].shape, 0)
    level = tiles
    for k in (1, 2, 4):
        turned = [pltpu.roll(v, 8 - k, 0) for v in level]
        after = turned[1:] + turned[-1:]
        level = [
            v + jnp.where(row < 8 - k, a, b) for v, a, b in zip(level, turned, after)
        ]
    return [level[j] + level[j + 1] + tiles[j + 2] for j in range(count - 2)]


def box(tiles, band, joint):
    return along_rows(along_lanes(tiles, band, joint))


def smooth_body(
    wide, turn, in_ref, band_ref, joint_ref, s_ref, e_ref, life_ref, inverse_ref, scale_ref
):
    parts = in_ref.shape[0]
    half = LANES // 2
    total = inverse_ref.shape[0] + 2 * RADIUS
    share = total - 2 * HALO
    left = lax.broadcasted_iota(jnp.int32, (total, LANES), 1) < half
    weights, fields = [], []
    for t in range(0, parts, 2):
        a = in_ref[t, :total, :]
        b = in_ref[t + 1, :total, :]
        weights.append(jnp.where(left, a, pltpu.roll(b, half, 1)))
        fields.append(jnp.where(left, pltpu.roll(a, half, 1), b))
    weight = jnp.concatenate(weights, axis=1)
    field = jnp.concatenate(fields, axis=1)

    sections = lax.axis_size("gz")
    first = lax.rem(lax.axis_index("gz") + sections - turn, sections) * wide
    left = lax.broadcasted_iota(jnp.int32, (1, LANES), 1) < half
    for i in range(wide):
        pair = 2 * jnp.minimum((first + i) // share, parts // 2 - 1)
        a = in_ref[pair, total + i:total + i + 1, :]
        b = in_ref[pair + 1, total + i:total + i + 1, :]
        life_ref[i:i + 1, :] = jnp.where(left, a, b)

    band = band_ref[...]
    joint = joint_ref[...]
    weights = [weight[r:r + 8] for r in range(0, total, 8)]
    now = [w * field[8 * j:8 * j + 8] for j, w in enumerate(weights)]
    denoms = box(weights, band, joint)
    inverse = [1.0 / jnp.maximum(d, 1.0) for d in denoms]
    for j, value in enumerate(inverse):
        inverse_ref[8 * j:8 * j + 8, :] = value
        scale_ref[8 * j:8 * j + 8, :] = value * weights[j + 1]
    for level in range(PASSES):
        now = box(now, band, joint)
        factor = scale_ref if level < PASSES - 1 else inverse_ref
        now = [
            v * factor[8 * (j + level):8 * (j + level + 1), :] for j, v in enumerate(now)
        ]
    smoothed = jnp.concatenate(now, axis=0)
    rest = field[HALO:HALO + share] - smoothed
    for c in range(parts // 2):
        s_ref[c * share:(c + 1) * share, :] = smoothed[:, c * LANES:(c + 1) * LANES]
        e_ref[c * share:(c + 1) * share, :] = rest[:, c * LANES:(c + 1) * LANES]
    used = e_ref.shape[0]
    s_ref[used:, :] = jnp.zeros((s_ref.shape[0] - used, LANES), F32)


def norms_body(keep_ref, life_ref, fade_ref, fore_ref, back_ref):
    sections = keep_ref.shape[0]
    wide = life_ref.shape[0]
    fade = jnp.exp(-life_ref[...] / sections)
    fade_ref[...] = fade
    norm = jnp.zeros_like(fade)
    for z in range(sections):
        decay = keep_ref[z] * fade
        gain = 1.0 - decay
        norm = decay * norm + gain
        fore_ref[z * wide:(z + 1) * wide, :] = gain / norm
    norm = jnp.zeros_like(fade)
    for z in reversed(range(sections)):
        decay = keep_ref[z] * fade
        norm = decay * norm + (1.0 - decay)
        back_ref[z * wide:(z + 1) * wide, :] = 1.0 / norm


def scan_body(turn, keep_ref, fade_ref, fore_ref, back_ref, s_ref, out_ref):
    sections = keep_ref.shape[0]
    wide = fade_ref.shape[0]
    fade = fade_ref[...]
    mass = jnp.zeros_like(fade)

    def rows(z):
        return slice(z * wide, (z + 1) * wide)

    for z in range(sections):
        decay = keep_ref[z] * fade
        at = rows((z - turn) % sections)
        mass = decay * mass + (1.0 - decay) * s_ref[at, :]
        out_ref[at, :] = mass * fore_ref[rows(z), :]
    mass = jnp.zeros_like(fade)
    for z in reversed(range(sections)):
        decay = keep_ref[z] * fade
        at = rows((z - turn) % sections)
        mass = decay * mass + out_ref[at, :]
        out_ref[at, :] = mass * back_ref[rows(z), :]


def finish_body(e_ref, drift_ref, out_ref):
    share = out_ref.shape[0]
    for c in range(out_ref.shape[1] // LANES):
        at = slice(c * share, (c + 1) * share)
        out_ref[:, c * LANES:(c + 1) * LANES] = e_ref[at, :] + drift_ref[at, :]


def call(body, name, outs, ins, scratch=()):
    return pl.pallas_call(
        body,
        out_shape=outs,
        in_specs=ins,
        out_specs=jax.tree.map(lambda _: VM, outs),
        scratch_shapes=scratch,
        compiler_params=PARAMS,
        name=name,
    )


def in_hbm(values):
    return pltpu.with_memory_space_constraint(values, pltpu.HBM)


def shape(*dims):
    return jax.ShapeDtypeStruct(dims, F32)


def shards(log_mean, tile_mask, coverage, lifetime, keep):
    rows, cols = log_mean.shape[1:]
    sections = keep.shape[0]
    parts = lax.axis_size("ta")
    share = cols // parts
    total = share + 2 * HALO
    used = rows * cols // LANES
    wide = -(-used // sections)
    padded = sections * wide
    turn = START % sections

    sent = call(
        lambda *refs: prepare_body(wide, turn, *refs),
        "prepare",
        shape(parts, total + 8, LANES),
        [HB] * 4,
        [pltpu.VMEM((rows, cols), a.dtype) for a in (log_mean, tile_mask, coverage, lifetime)]
        + [pltpu.VMEM((cols + 2 * HALO, LANES), F32), pltpu.VMEM((cols, LANES), F32)]
        + [pltpu.SemaphoreType.DMA((4,))],
    )(*(in_hbm(a) for a in (log_mean[0], tile_mask[0], coverage[0], lifetime)))
    sent = lax.all_to_all(sent, "ta", 0, 0, tiled=True)

    half = np.arange(rows * parts // 2)
    near = np.abs(half[:, None] - half[None, :]) <= RADIUS
    left = half < half.size // 2
    band = near.astype(BF16)
    joint = (near & (left[:, None] != left[None, :])).astype(BF16)
    smoothed, rest, life = call(
        lambda *refs: smooth_body(wide, turn, *refs),
        "smooth",
        (shape(padded, LANES), shape(used, LANES), shape(wide, LANES)),
        [VM] * 3,
        [pltpu.VMEM((total - 2 * RADIUS, rows * parts), F32)] * 2,
    )(sent, band, joint)

    order = [(i + turn) % sections for i in range(sections)]

    def swap(values):
        flat = values.reshape(padded * LANES)
        flat = lax.all_to_all(flat, "gz", 0, 0, tiled=True, axis_index_groups=[order])
        return flat.reshape(padded, LANES)

    long = shape(padded, LANES)
    fade, fore, back = call(
        norms_body, "norms", (shape(wide, LANES), long, long), [SM, VM]
    )(keep, life)
    drift = call(lambda *refs: scan_body(turn, *refs), "scan", long, [SM] + [VM] * 4)(
        keep, fade, fore, back, swap(smoothed)
    )
    out = call(finish_body, "finish", shape(share, rows * parts), [VM] * 2)(rest, swap(drift))
    return out.T[None]


def solution(mesh):
    return jax.shard_map(
        shards,
        mesh=mesh,
        in_specs=(
            P("gz", "ta", None),
            P("gz", "ta", None),
            P("gz", "ta", None),
            P("ta", None),
            P(),
        ),
        out_specs=P("gz", None, "ta"),
        check_vma=False,
    )
```

```python
import jax
import jax.numpy as jnp
import numpy as np
from jax import lax
from jax.experimental import pallas as pl
from jax.experimental.pallas import tpu as pltpu
from jax.sharding import PartitionSpec as P

RADIUS = 8
PASSES = 7
HALO = RADIUS * PASSES
START = 67
FIRST = 7
LANES = 128
F32 = jnp.float32
BF16 = jnp.bfloat16
VM = pl.BlockSpec(memory_space=pltpu.VMEM)
HB = pl.BlockSpec(memory_space=pltpu.HBM)
SM = pl.BlockSpec(memory_space=pltpu.SMEM)
PARAMS = pltpu.CompilerParams(vmem_limit_bytes=16 << 20)


def prepare_body(
    wide, turn, log_hbm, mask_hbm, cov_hbm, life_hbm, out_ref,
    log_ref, mask_ref, cov_ref, life_ref, both_ref, life_t_ref, sems,
):
    pairs = ((life_hbm, life_ref), (log_hbm, log_ref), (mask_hbm, mask_ref), (cov_hbm, cov_ref))
    copies = [pltpu.make_async_copy(a, b, sems.at[i]) for i, (a, b) in enumerate(pairs)]
    for copy in copies:
        copy.start()
    rows, cols = log_ref.shape
    parts, depth, _ = out_ref.shape
    share = cols // parts
    span = share + 2 * HALO
    both_ref[:HALO, :] = jnp.zeros((HALO, LANES), F32)
    both_ref[HALO + cols:, :] = jnp.zeros((HALO, LANES), F32)
    copies[0].wait()
    life = jnp.concatenate([life_ref[...], life_ref[...]], axis=0)
    for c in range(0, cols, LANES):
        life_t_ref[c:c + LANES, :] = life[:, c:c + LANES].T
    for copy in copies[1:]:
        copy.wait()
    weight = 1.0 + mask_ref[...].astype(F32) * cov_ref[...].astype(F32)
    both = jnp.concatenate([weight, log_ref[...]], axis=0)
    for c in range(0, cols, LANES):
        both_ref[HALO + c:HALO + c + LANES, :] = both[:, c:c + LANES].T
    sections = lax.axis_size("gz")
    first = lax.rem(lax.axis_index("gz") + sections - turn, sections) * wide
    for t in range(parts):
        slot = (t - FIRST) % parts
        out_ref[slot, :span, :] = both_ref[share * t:share * t + span, :]
        out_ref[slot, span:, :] = jnp.zeros((depth - span, LANES), F32)
        for i in range(wide):
            place = share * t + (first + i) % share
            out_ref[slot, span + i:span + i + 1, :] = life_t_ref[pl.ds(place, 1), :]


def halves(values):
    high = values.astype(BF16)
    return high, (values - high.astype(F32)).astype(BF16)


def dot(a, b):
    return jnp.dot(a, b, preferred_element_type=F32)


def along_lanes(tiles, band, joint):
    values = jnp.concatenate(tiles, axis=0)
    rows = values.shape[0]
    half = band.shape[0]
    edge = half // 2
    both = jnp.concatenate(halves(values), axis=0)
    sides = dot(jnp.concatenate([both[:, :half], both[:, half:]], axis=0), band)
    left, right = sides[:2 * rows], sides[2 * rows:]
    across = dot(both[:, edge:half + edge], joint)
    both = jnp.concatenate(
        [
            left[:, :edge],
            left[:, edge:] + across[:, :edge],
            right[:, :edge] + across[:, edge:],
            right[:, edge:],
        ],
        axis=1,
    )
    sums = both[:rows] + both[rows:]
    return [sums[r:r + 8] for r in range(0, rows, 8)]


def along_rows(tiles):
    count = len(tiles)
    row = lax.broadcasted_iota(jnp.int32, tiles[0].shape, 0)
    level = tiles
    for k in (1, 2, 4):
        turned = [pltpu.roll(v, 8 - k, 0) for v in level]
        after = turned[1:] + turned[-1:]
        level = [
            v + jnp.where(row < 8 - k, a, b) for v, a, b in zip(level, turned, after)
        ]
    return [level[j] + level[j + 1] + tiles[j + 2] for j in range(count - 2)]


def box(tiles, band, joint):
    return along_rows(along_lanes(tiles, band, joint))


def smooth_body(
    wide, turn, in_ref, band_ref, joint_ref, s_ref, e_ref, life_ref, inverse_ref, scale_ref
):
    parts = in_ref.shape[0]
    half = LANES // 2
    total = inverse_ref.shape[0] + 2 * RADIUS
    share = total - 2 * HALO
    left = lax.broadcasted_iota(jnp.int32, (total, LANES), 1) < half
    weights, fields = [], []
    for t in range(0, parts, 2):
        a = in_ref[(t - FIRST) % parts, :total, :]
        b = in_ref[(t + 1 - FIRST) % parts, :total, :]
        weights.append(jnp.where(left, a, pltpu.roll(b, half, 1)))
        fields.append(jnp.where(left, pltpu.roll(a, half, 1), b))
    weight = jnp.concatenate(weights, axis=1)
    field = jnp.concatenate(fields, axis=1)

    sections = lax.axis_size("gz")
    first = lax.rem(lax.axis_index("gz") + sections - turn, sections) * wide
    left = lax.broadcasted_iota(jnp.int32, (1, LANES), 1) < half
    for i in range(wide):
        pair = 2 * jnp.minimum((first + i) // share, parts // 2 - 1)
        shift = parts - FIRST
        a = in_ref[lax.rem(pair + shift, parts), total + i:total + i + 1, :]
        b = in_ref[lax.rem(pair + 1 + shift, parts), total + i:total + i + 1, :]
        life_ref[i:i + 1, :] = jnp.where(left, a, b)

    band = band_ref[...]
    joint = joint_ref[...]
    weights = [weight[r:r + 8] for r in range(0, total, 8)]
    now = [w * field[8 * j:8 * j + 8] for j, w in enumerate(weights)]
    denoms = box(weights, band, joint)
    inverse = [1.0 / jnp.maximum(d, 1.0) for d in denoms]
    for j, value in enumerate(inverse):
        inverse_ref[8 * j:8 * j + 8, :] = value
        scale_ref[8 * j:8 * j + 8, :] = value * weights[j + 1]
    for level in range(PASSES):
        now = box(now, band, joint)
        factor = scale_ref if level < PASSES - 1 else inverse_ref
        now = [
            v * factor[8 * (j + level):8 * (j + level + 1), :] for j, v in enumerate(now)
        ]
    smoothed = jnp.concatenate(now, axis=0)
    rest = field[HALO:HALO + share] - smoothed
    for c in range(parts // 2):
        s_ref[c * share:(c + 1) * share, :] = smoothed[:, c * LANES:(c + 1) * LANES]
        e_ref[c * share:(c + 1) * share, :] = rest[:, c * LANES:(c + 1) * LANES]
    used = e_ref.shape[0]
    s_ref[used:, :] = jnp.zeros((s_ref.shape[0] - used, LANES), F32)


def norms_body(keep_ref, life_ref, fade_ref, fore_ref, back_ref):
    sections = keep_ref.shape[0]
    wide = life_ref.shape[0]
    fade = jnp.exp(-life_ref[...] / sections)
    fade_ref[...] = fade
    norm = jnp.zeros_like(fade)
    for z in range(sections):
        decay = keep_ref[z] * fade
        gain = 1.0 - decay
        norm = decay * norm + gain
        fore_ref[z * wide:(z + 1) * wide, :] = gain / norm
    norm = jnp.zeros_like(fade)
    for z in reversed(range(sections)):
        decay = keep_ref[z] * fade
        norm = decay * norm + (1.0 - decay)
        back_ref[z * wide:(z + 1) * wide, :] = 1.0 / norm


def scan_body(turn, keep_ref, fade_ref, fore_ref, back_ref, s_ref, out_ref):
    sections = keep_ref.shape[0]
    wide = fade_ref.shape[0]
    fade = fade_ref[...]
    mass = jnp.zeros_like(fade)

    def rows(z):
        return slice(z * wide, (z + 1) * wide)

    for z in range(sections):
        decay = keep_ref[z] * fade
        mass = decay * mass + (1.0 - decay) * s_ref[rows((z - turn) % sections), :]
        out_ref[rows((z - turn) % sections), :] = mass * fore_ref[rows(z), :]
    mass = jnp.zeros_like(fade)
    for z in reversed(range(sections)):
        decay = keep_ref[z] * fade
        at = rows((z - turn) % sections)
        mass = decay * mass + out_ref[at, :]
        out_ref[at, :] = mass * back_ref[rows(z), :]


def finish_body(e_ref, drift_ref, out_ref):
    share = out_ref.shape[0]
    for c in range(out_ref.shape[1] // LANES):
        at = slice(c * share, (c + 1) * share)
        out_ref[:, c * LANES:(c + 1) * LANES] = e_ref[at, :] + drift_ref[at, :]


def call(body, name, outs, ins, scratch=()):
    return pl.pallas_call(
        body,
        out_shape=outs,
        in_specs=ins,
        out_specs=jax.tree.map(lambda _: VM, outs),
        scratch_shapes=scratch,
        compiler_params=PARAMS,
        name=name,
    )


def in_hbm(values):
    return pltpu.with_memory_space_constraint(values, pltpu.HBM)


def shape(*dims):
    return jax.ShapeDtypeStruct(dims, F32)


def shards(log_mean, tile_mask, coverage, lifetime, keep):
    rows, cols = log_mean.shape[1:]
    sections = keep.shape[0]
    parts = lax.axis_size("ta")
    share = cols // parts
    total = share + 2 * HALO
    used = rows * cols // LANES
    wide = -(-used // sections)
    padded = sections * wide
    turn = START % sections

    sent = call(
        lambda *refs: prepare_body(wide, turn, *refs),
        "prepare",
        shape(parts, total + 8, LANES),
        [HB] * 4,
        [pltpu.VMEM((rows, cols), a.dtype) for a in (log_mean, tile_mask, coverage, lifetime)]
        + [pltpu.VMEM((cols + 2 * HALO, LANES), F32), pltpu.VMEM((cols, LANES), F32)]
        + [pltpu.SemaphoreType.DMA((4,))],
    )(*(in_hbm(a) for a in (log_mean[0], tile_mask[0], coverage[0], lifetime)))
    ring = [(i + FIRST) % parts for i in range(parts)]
    sent = lax.all_to_all(sent, "ta", 0, 0, tiled=True, axis_index_groups=[ring])

    half = np.arange(rows * parts // 2)
    near = np.abs(half[:, None] - half[None, :]) <= RADIUS
    left = half < half.size // 2
    band = near.astype(BF16)
    joint = (near & (left[:, None] != left[None, :])).astype(BF16)
    smoothed, rest, life = call(
        lambda *refs: smooth_body(wide, turn, *refs),
        "smooth",
        (shape(padded, LANES), shape(used, LANES), shape(wide, LANES)),
        [VM] * 3,
        [pltpu.VMEM((total - 2 * RADIUS, rows * parts), F32)] * 2,
    )(sent, band, joint)

    order = [(i + turn) % sections for i in range(sections)]

    def swap(values):
        flat = values.reshape(padded * LANES)
        flat = lax.all_to_all(flat, "gz", 0, 0, tiled=True, axis_index_groups=[order])
        return flat.reshape(padded, LANES)

    long = shape(padded, LANES)
    fade, fore, back = call(
        norms_body, "norms", (shape(wide, LANES), long, long), [SM, VM]
    )(keep, life)
    drift = call(lambda *refs: scan_body(turn, *refs), "scan", long, [SM] + [VM] * 4)(
        keep, fade, fore, back, swap(smoothed)
    )
    out = call(finish_body, "finish", shape(share, rows * parts), [VM] * 2)(rest, swap(drift))
    return out.T[None]


def solution(mesh):
    return jax.shard_map(
        shards,
        mesh=mesh,
        in_specs=(
            P("gz", "ta", None),
            P("gz", "ta", None),
            P("gz", "ta", None),
            P("ta", None),
            P(),
        ),
        out_specs=P("gz", None, "ta"),
        check_vma=False,
    )
```

```python
import jax
import jax.numpy as jnp
import numpy as np
from jax import lax
from jax.experimental import pallas as pl
from jax.experimental.pallas import tpu as pltpu
from jax.sharding import PartitionSpec as P

RADIUS = 8
PASSES = 7
HALO = RADIUS * PASSES
START = 67
FIRST = 7
SPANS = 4
LANES = 128
F32 = jnp.float32
BF16 = jnp.bfloat16
VM = pl.BlockSpec(memory_space=pltpu.VMEM)
HB = pl.BlockSpec(memory_space=pltpu.HBM)
SM = pl.BlockSpec(memory_space=pltpu.SMEM)
PARAMS = pltpu.CompilerParams(vmem_limit_bytes=16 << 20)


def prepare_body(
    wide, turn, log_hbm, mask_hbm, cov_hbm, life_hbm, out_ref,
    log_ref, mask_ref, cov_ref, life_ref, both_ref, life_t_ref, sems,
):
    pairs = ((life_hbm, life_ref), (log_hbm, log_ref), (mask_hbm, mask_ref), (cov_hbm, cov_ref))
    copies = [pltpu.make_async_copy(a, b, sems.at[i]) for i, (a, b) in enumerate(pairs)]
    for copy in copies:
        copy.start()
    rows, cols = log_ref.shape
    parts, depth, _ = out_ref.shape
    share = cols // parts
    span = share + 2 * HALO
    both_ref[:HALO, :] = jnp.zeros((HALO, LANES), F32)
    both_ref[HALO + cols:, :] = jnp.zeros((HALO, LANES), F32)
    copies[0].wait()
    life = jnp.concatenate([life_ref[...], life_ref[...]], axis=0)
    for c in range(0, cols, LANES):
        life_t_ref[c:c + LANES, :] = life[:, c:c + LANES].T
    for copy in copies[1:]:
        copy.wait()
    weight = 1.0 + mask_ref[...].astype(F32) * cov_ref[...].astype(F32)
    both = jnp.concatenate([weight, log_ref[...]], axis=0)
    for c in range(0, cols, LANES):
        both_ref[HALO + c:HALO + c + LANES, :] = both[:, c:c + LANES].T
    sections = lax.axis_size("gz")
    first = lax.rem(lax.axis_index("gz") + sections - turn, sections) * wide
    for t in range(parts):
        slot = (t - FIRST) % parts
        out_ref[slot, :span, :] = both_ref[share * t:share * t + span, :]
        out_ref[slot, span:, :] = jnp.zeros((depth - span, LANES), F32)
        for i in range(wide):
            place = share * t + (first + i) % share
            out_ref[slot, span + i:span + i + 1, :] = life_t_ref[pl.ds(place, 1), :]


def halves(values):
    high = values.astype(BF16)
    return high, (values - high.astype(F32)).astype(BF16)


def dot(a, b):
    return jnp.dot(a, b, preferred_element_type=F32)


def along_lanes(tiles, band, joint):
    values = jnp.concatenate(tiles, axis=0)
    rows = values.shape[0]
    half = band.shape[0]
    edge = half // 2
    both = jnp.concatenate(halves(values), axis=0)
    sides = dot(jnp.concatenate([both[:, :half], both[:, half:]], axis=0), band)
    left = sides[:rows] + sides[rows:2 * rows]
    right = sides[2 * rows:3 * rows] + sides[3 * rows:]
    near = lax.broadcasted_iota(jnp.int32, (rows, edge), 1) < edge // 2
    middle = jnp.where(near, values[:, half:half + edge], values[:, edge:half])
    across = dot(jnp.concatenate(halves(middle), axis=1), joint)
    sums = jnp.concatenate(
        [
            left[:, :edge],
            left[:, edge:] + across[:, :edge],
            right[:, :edge] + across[:, edge:],
            right[:, edge:],
        ],
        axis=1,
    )
    return [sums[r:r + 8] for r in range(0, rows, 8)]


def along_rows(tiles):
    count = len(tiles)
    row = lax.broadcasted_iota(jnp.int32, tiles[0].shape, 0)
    level = tiles
    for k in (1, 2, 4):
        turned = [pltpu.roll(v, 8 - k, 0) for v in level]
        after = turned[1:] + turned[-1:]
        level = [
            v + jnp.where(row < 8 - k, a, b) for v, a, b in zip(level, turned, after)
        ]
    return [level[j] + level[j + 1] + tiles[j + 2] for j in range(count - 2)]


def smooth_body(
    wide, turn, in_ref, band_ref, joint_ref, s_ref, e_ref, life_ref, inverse_ref, scale_ref
):
    parts = in_ref.shape[0]
    half = LANES // 2
    total = inverse_ref.shape[0] + 2 * RADIUS
    share = total - 2 * HALO
    left = lax.broadcasted_iota(jnp.int32, (total, LANES), 1) < half
    weights, fields = [], []
    for t in range(0, parts, 2):
        a = in_ref[(t - FIRST) % parts, :total, :]
        b = in_ref[(t + 1 - FIRST) % parts, :total, :]
        weights.append(jnp.where(left, a, pltpu.roll(b, half, 1)))
        fields.append(jnp.where(left, pltpu.roll(a, half, 1), b))
    weight = jnp.concatenate(weights, axis=1)
    field = jnp.concatenate(fields, axis=1)

    sections = lax.axis_size("gz")
    first = lax.rem(lax.axis_index("gz") + sections - turn, sections) * wide
    left = lax.broadcasted_iota(jnp.int32, (1, LANES), 1) < half
    for i in range(wide):
        pair = 2 * jnp.minimum((first + i) // share, parts // 2 - 1)
        shift = parts - FIRST
        a = in_ref[lax.rem(pair + shift, parts), total + i:total + i + 1, :]
        b = in_ref[lax.rem(pair + 1 + shift, parts), total + i:total + i + 1, :]
        life_ref[i:i + 1, :] = jnp.where(left, a, b)

    band = band_ref[...]
    joint = joint_ref[...]
    weights = [weight[r:r + 8] for r in range(0, total, 8)]
    now = [w * field[8 * j:8 * j + 8] for j, w in enumerate(weights)]
    denoms = along_rows(along_lanes(weights, band, joint))
    inverse = [1.0 / jnp.maximum(d, 1.0) for d in denoms]
    for j, value in enumerate(inverse):
        inverse_ref[8 * j:8 * j + 8, :] = value
        scale_ref[8 * j:8 * j + 8, :] = value * weights[j + 1]
    for level in range(PASSES):
        now = along_rows(along_lanes(now, band, joint))
        factor = scale_ref if level < PASSES - 1 else inverse_ref
        now = [
            v * factor[8 * (j + level):8 * (j + level + 1), :] for j, v in enumerate(now)
        ]
    smoothed = jnp.concatenate(now, axis=0)
    rest = field[HALO:HALO + share] - smoothed
    for c in range(parts // 2):
        s_ref[c * share:(c + 1) * share, :] = smoothed[:, c * LANES:(c + 1) * LANES]
        e_ref[c * share:(c + 1) * share, :] = rest[:, c * LANES:(c + 1) * LANES]
    used = e_ref.shape[0]
    s_ref[used:, :] = jnp.zeros((s_ref.shape[0] - used, LANES), F32)


def norms_body(
    keep_ref, life_ref, fade_ref, fore_ref, back_ref, fore_lead_ref, back_lead_ref, ends_ref
):
    sections = keep_ref.shape[0]
    wide = life_ref.shape[0]
    run = sections // SPANS
    fade = jnp.exp(-life_ref[...] / sections)
    fade_ref[...] = fade
    norm = jnp.zeros_like(fade)
    lead = jnp.ones_like(fade)
    for z in range(sections):
        at = slice(z * wide, (z + 1) * wide)
        decay = keep_ref[z] * fade
        gain = 1.0 - decay
        norm = decay * norm + gain
        lead = lead * decay if z % run else decay
        share = gain / norm
        fore_ref[at, :] = share
        fore_lead_ref[at, :] = lead * share
        if z % run == run - 1:
            ends_ref[z // run * wide:(z // run + 1) * wide, :] = lead
    norm = jnp.zeros_like(fade)
    for z in reversed(range(sections)):
        at = slice(z * wide, (z + 1) * wide)
        decay = keep_ref[z] * fade
        norm = decay * norm + (1.0 - decay)
        lead = lead * decay if (z + 1) % run else decay
        share = 1.0 / norm
        back_ref[at, :] = share
        back_lead_ref[at, :] = lead * share


def scan_body(
    turn, keep_ref, fade_ref, fore_ref, back_ref, fore_lead_ref, back_lead_ref, ends_ref,
    s_ref, out_ref,
):
    sections = keep_ref.shape[0]
    wide = fade_ref.shape[0]
    fade = fade_ref[...]
    run = sections // SPANS
    zero = jnp.zeros_like(fade)

    def rows(z):
        return slice(z * wide, (z + 1) * wide)

    def seat(z):
        return rows((z - turn) % sections)

    ends = [ends_ref[rows(k), :] for k in range(SPANS)]
    mass = [zero] * SPANS
    for i in range(run):
        for k in range(SPANS):
            z = k * run + i
            decay = keep_ref[z] * fade
            mass[k] = decay * mass[k] + (1.0 - decay) * s_ref[seat(z), :]
            out_ref[seat(z), :] = mass[k] * fore_ref[rows(z), :]
    carry = [zero]
    for k in range(SPANS - 1):
        carry.append(mass[k] + ends[k] * carry[k])
    mass = [zero] * SPANS
    for i in reversed(range(run)):
        for k in range(SPANS):
            z = k * run + i
            decay = keep_ref[z] * fade
            value = out_ref[seat(z), :] + fore_lead_ref[rows(z), :] * carry[k]
            mass[k] = decay * mass[k] + value
            out_ref[seat(z), :] = mass[k] * back_ref[rows(z), :]
    carry = [zero] * SPANS
    for k in reversed(range(SPANS - 1)):
        carry[k] = mass[k + 1] + ends[k + 1] * carry[k + 1]
    for k in range(SPANS - 1):
        for i in range(run):
            z = k * run + i
            out_ref[seat(z), :] = out_ref[seat(z), :] + back_lead_ref[rows(z), :] * carry[k]


def finish_body(e_ref, drift_ref, out_ref):
    share = out_ref.shape[0]
    for c in range(out_ref.shape[1] // LANES):
        at = slice(c * share, (c + 1) * share)
        out_ref[:, c * LANES:(c + 1) * LANES] = e_ref[at, :] + drift_ref[at, :]


def call(body, name, outs, ins, scratch=()):
    return pl.pallas_call(
        body,
        out_shape=outs,
        in_specs=ins,
        out_specs=jax.tree.map(lambda _: VM, outs),
        scratch_shapes=scratch,
        compiler_params=PARAMS,
        name=name,
    )


def in_hbm(values):
    return pltpu.with_memory_space_constraint(values, pltpu.HBM)


def shape(*dims):
    return jax.ShapeDtypeStruct(dims, F32)


def shards(log_mean, tile_mask, coverage, lifetime, keep):
    rows, cols = log_mean.shape[1:]
    sections = keep.shape[0]
    parts = lax.axis_size("ta")
    share = cols // parts
    total = share + 2 * HALO
    used = rows * cols // LANES
    wide = -(-used // sections)
    padded = sections * wide
    turn = START % sections

    sent = call(
        lambda *refs: prepare_body(wide, turn, *refs),
        "prepare",
        shape(parts, total + 8, LANES),
        [HB] * 4,
        [pltpu.VMEM((rows, cols), a.dtype) for a in (log_mean, tile_mask, coverage, lifetime)]
        + [pltpu.VMEM((cols + 2 * HALO, LANES), F32), pltpu.VMEM((cols, LANES), F32)]
        + [pltpu.SemaphoreType.DMA((4,))],
    )(*(in_hbm(a) for a in (log_mean[0], tile_mask[0], coverage[0], lifetime)))
    ring = [(i + FIRST) % parts for i in range(parts)]
    sent = lax.all_to_all(sent, "ta", 0, 0, tiled=True, axis_index_groups=[ring])

    half = np.arange(rows * parts // 2)
    near = np.abs(half[:, None] - half[None, :]) <= RADIUS
    band = near.astype(BF16)
    edge = half.size // 2
    lane = np.arange(edge)
    source = np.tile(np.where(lane < edge // 2, lane + half.size, lane + edge), 2)
    target = half + edge
    joint = np.abs(source[:, None] - target[None, :]) <= RADIUS
    joint = joint & ((source < half.size)[:, None] != (target < half.size)[None, :])
    joint = joint.astype(BF16)
    smoothed, rest, life = call(
        lambda *refs: smooth_body(wide, turn, *refs),
        "smooth",
        (shape(padded, LANES), shape(used, LANES), shape(wide, LANES)),
        [VM] * 3,
        [pltpu.VMEM((total - 2 * RADIUS, rows * parts), F32)] * 2,
    )(sent, band, joint)

    order = [(i + turn) % sections for i in range(sections)]

    def swap(values):
        flat = values.reshape(padded * LANES)
        flat = lax.all_to_all(flat, "gz", 0, 0, tiled=True, axis_index_groups=[order])
        return flat.reshape(padded, LANES)

    long = shape(padded, LANES)
    tables = call(
        norms_body,
        "norms",
        (shape(wide, LANES), long, long, long, long, shape(SPANS * wide, LANES)),
        [SM, VM],
    )(keep, life)
    drift = call(lambda *refs: scan_body(turn, *refs), "scan", long, [SM] + [VM] * 7)(
        keep, *tables, swap(smoothed)
    )
    out = call(finish_body, "finish", shape(share, rows * parts), [VM] * 2)(rest, swap(drift))
    return out.T[None]


def solution(mesh):
    return jax.shard_map(
        shards,
        mesh=mesh,
        in_specs=(
            P("gz", "ta", None),
            P("gz", "ta", None),
            P("gz", "ta", None),
            P("ta", None),
            P(),
        ),
        out_specs=P("gz", None, "ta"),
        check_vma=False,
    )
```

```python
import jax
import jax.numpy as jnp
import numpy as np
from jax import lax
from jax.experimental import pallas as pl
from jax.experimental.pallas import tpu as pltpu
from jax.sharding import PartitionSpec as P

RADIUS = 8
PASSES = 7
HALO = RADIUS * PASSES
START = 67
FIRST = 7
SPANS = 4
DEPTH = 12
LANES = 128
F32 = jnp.float32
BF16 = jnp.bfloat16
VM = pl.BlockSpec(memory_space=pltpu.VMEM)
HB = pl.BlockSpec(memory_space=pltpu.HBM)
SM = pl.BlockSpec(memory_space=pltpu.SMEM)
PARAMS = pltpu.CompilerParams(vmem_limit_bytes=16 << 20)


def seat_of(g, turn, sections):
    high = sections // DEPTH
    level = (g % DEPTH + DEPTH - turn % DEPTH) % DEPTH
    return level * high + (g // DEPTH + high - turn // DEPTH) % high


def prepare_body(
    wide, turn, log_hbm, mask_hbm, cov_hbm, life_hbm, out_ref,
    log_ref, mask_ref, cov_ref, life_ref, both_ref, life_t_ref, sems,
):
    pairs = ((life_hbm, life_ref), (log_hbm, log_ref), (mask_hbm, mask_ref), (cov_hbm, cov_ref))
    copies = [pltpu.make_async_copy(a, b, sems.at[i]) for i, (a, b) in enumerate(pairs)]
    for copy in copies:
        copy.start()
    rows, cols = log_ref.shape
    parts, depth, _ = out_ref.shape
    share = cols // parts
    span = share + 2 * HALO
    both_ref[:HALO, :] = jnp.zeros((HALO, LANES), F32)
    both_ref[HALO + cols:, :] = jnp.zeros((HALO, LANES), F32)
    copies[0].wait()
    life = jnp.concatenate([life_ref[...], life_ref[...]], axis=0)
    for c in range(0, cols, LANES):
        life_t_ref[c:c + LANES, :] = life[:, c:c + LANES].T
    for copy in copies[1:]:
        copy.wait()
    weight = 1.0 + mask_ref[...].astype(F32) * cov_ref[...].astype(F32)
    both = jnp.concatenate([weight, log_ref[...]], axis=0)
    for c in range(0, cols, LANES):
        both_ref[HALO + c:HALO + c + LANES, :] = both[:, c:c + LANES].T
    sections = lax.axis_size("gz")
    first = seat_of(lax.axis_index("gz"), turn, sections) * wide
    for t in range(parts):
        slot = (t - FIRST) % parts
        out_ref[slot, :span, :] = both_ref[share * t:share * t + span, :]
        out_ref[slot, span:, :] = jnp.zeros((depth - span, LANES), F32)
        for i in range(wide):
            place = share * t + (first + i) % share
            out_ref[slot, span + i:span + i + 1, :] = life_t_ref[pl.ds(place, 1), :]


def halves(values):
    high = values.astype(BF16)
    return high, (values - high.astype(F32)).astype(BF16)


def dot(a, b):
    return jnp.dot(a, b, preferred_element_type=F32)


def along_lanes(tiles, band, joint):
    values = jnp.concatenate(tiles, axis=0)
    rows = values.shape[0]
    half = band.shape[0]
    edge = half // 2
    both = jnp.concatenate(halves(values), axis=0)
    sides = dot(jnp.concatenate([both[:, :half], both[:, half:]], axis=0), band)
    left = sides[:rows] + sides[rows:2 * rows]
    right = sides[2 * rows:3 * rows] + sides[3 * rows:]
    near = lax.broadcasted_iota(jnp.int32, (rows, edge), 1) < edge // 2
    middle = jnp.where(near, values[:, half:half + edge], values[:, edge:half])
    across = dot(jnp.concatenate(halves(middle), axis=1), joint)
    sums = jnp.concatenate(
        [
            left[:, :edge],
            left[:, edge:] + across[:, :edge],
            right[:, :edge] + across[:, edge:],
            right[:, edge:],
        ],
        axis=1,
    )
    return [sums[r:r + 8] for r in range(0, rows, 8)]


def along_rows(tiles):
    count = len(tiles)
    row = lax.broadcasted_iota(jnp.int32, tiles[0].shape, 0)
    level = tiles
    for k in (1, 2, 4):
        turned = [pltpu.roll(v, 8 - k, 0) for v in level]
        after = turned[1:] + turned[-1:]
        level = [
            v + jnp.where(row < 8 - k, a, b) for v, a, b in zip(level, turned, after)
        ]
    return [level[j] + level[j + 1] + tiles[j + 2] for j in range(count - 2)]


def smooth_body(
    wide, turn, in_ref, band_ref, joint_ref, s_ref, e_ref, life_ref, inverse_ref, scale_ref
):
    parts = in_ref.shape[0]
    half = LANES // 2
    total = inverse_ref.shape[0] + 2 * RADIUS
    share = total - 2 * HALO
    left = lax.broadcasted_iota(jnp.int32, (total, LANES), 1) < half
    weights, fields = [], []
    for t in range(0, parts, 2):
        a = in_ref[(t - FIRST) % parts, :total, :]
        b = in_ref[(t + 1 - FIRST) % parts, :total, :]
        weights.append(jnp.where(left, a, pltpu.roll(b, half, 1)))
        fields.append(jnp.where(left, pltpu.roll(a, half, 1), b))
    weight = jnp.concatenate(weights, axis=1)
    field = jnp.concatenate(fields, axis=1)

    sections = lax.axis_size("gz")
    first = seat_of(lax.axis_index("gz"), turn, sections) * wide
    left = lax.broadcasted_iota(jnp.int32, (1, LANES), 1) < half
    for i in range(wide):
        pair = 2 * jnp.minimum((first + i) // share, parts // 2 - 1)
        shift = parts - FIRST
        a = in_ref[lax.rem(pair + shift, parts), total + i:total + i + 1, :]
        b = in_ref[lax.rem(pair + 1 + shift, parts), total + i:total + i + 1, :]
        life_ref[i:i + 1, :] = jnp.where(left, a, b)

    band = band_ref[...]
    joint = joint_ref[...]
    weights = [weight[r:r + 8] for r in range(0, total, 8)]
    now = [w * field[8 * j:8 * j + 8] for j, w in enumerate(weights)]
    denoms = along_rows(along_lanes(weights, band, joint))
    inverse = [1.0 / jnp.maximum(d, 1.0) for d in denoms]
    for j, value in enumerate(inverse):
        inverse_ref[8 * j:8 * j + 8, :] = value
        scale_ref[8 * j:8 * j + 8, :] = value * weights[j + 1]
    for level in range(PASSES):
        now = along_rows(along_lanes(now, band, joint))
        factor = scale_ref if level < PASSES - 1 else inverse_ref
        now = [
            v * factor[8 * (j + level):8 * (j + level + 1), :] for j, v in enumerate(now)
        ]
    smoothed = jnp.concatenate(now, axis=0)
    rest = field[HALO:HALO + share] - smoothed
    for c in range(parts // 2):
        s_ref[c * share:(c + 1) * share, :] = smoothed[:, c * LANES:(c + 1) * LANES]
        e_ref[c * share:(c + 1) * share, :] = rest[:, c * LANES:(c + 1) * LANES]
    used = e_ref.shape[0]
    s_ref[used:, :] = jnp.zeros((s_ref.shape[0] - used, LANES), F32)


def norms_body(
    keep_ref, life_ref, fade_ref, fore_ref, back_ref, fore_lead_ref, back_lead_ref, ends_ref
):
    sections = keep_ref.shape[0]
    wide = life_ref.shape[0]
    run = sections // SPANS
    fade = jnp.exp(-life_ref[...] / sections)
    fade_ref[...] = fade
    norm = jnp.zeros_like(fade)
    lead = jnp.ones_like(fade)
    for z in range(sections):
        at = slice(z * wide, (z + 1) * wide)
        decay = keep_ref[z] * fade
        gain = 1.0 - decay
        norm = decay * norm + gain
        lead = lead * decay if z % run else decay
        share = gain / norm
        fore_ref[at, :] = share
        fore_lead_ref[at, :] = lead * share
        if z % run == run - 1:
            ends_ref[z // run * wide:(z // run + 1) * wide, :] = lead
    norm = jnp.zeros_like(fade)
    for z in reversed(range(sections)):
        at = slice(z * wide, (z + 1) * wide)
        decay = keep_ref[z] * fade
        norm = decay * norm + (1.0 - decay)
        lead = lead * decay if (z + 1) % run else decay
        share = 1.0 / norm
        back_ref[at, :] = share
        back_lead_ref[at, :] = lead * share


def scan_body(
    turn, keep_ref, fade_ref, fore_ref, back_ref, fore_lead_ref, back_lead_ref, ends_ref,
    s_ref, out_ref,
):
    sections = keep_ref.shape[0]
    wide = fade_ref.shape[0]
    fade = fade_ref[...]
    run = sections // SPANS
    zero = jnp.zeros_like(fade)

    def rows(z):
        return slice(z * wide, (z + 1) * wide)

    def seat(z):
        return rows(seat_of(z, turn, sections))

    ends = [ends_ref[rows(k), :] for k in range(SPANS)]
    mass = [zero] * SPANS
    for i in range(run):
        for k in range(SPANS):
            z = k * run + i
            decay = keep_ref[z] * fade
            mass[k] = decay * mass[k] + (1.0 - decay) * s_ref[seat(z), :]
            out_ref[seat(z), :] = mass[k] * fore_ref[rows(z), :]
    carry = [zero]
    for k in range(SPANS - 1):
        carry.append(mass[k] + ends[k] * carry[k])
    mass = [zero] * SPANS
    for i in reversed(range(run)):
        for k in range(SPANS):
            z = k * run + i
            decay = keep_ref[z] * fade
            value = out_ref[seat(z), :] + fore_lead_ref[rows(z), :] * carry[k]
            mass[k] = decay * mass[k] + value
            out_ref[seat(z), :] = mass[k] * back_ref[rows(z), :]
    carry = [zero] * SPANS
    for k in reversed(range(SPANS - 1)):
        carry[k] = mass[k + 1] + ends[k + 1] * carry[k + 1]
    for k in range(SPANS - 1):
        for i in range(run):
            z = k * run + i
            out_ref[seat(z), :] = out_ref[seat(z), :] + back_lead_ref[rows(z), :] * carry[k]


def finish_body(e_ref, drift_ref, out_ref):
    share = out_ref.shape[0]
    for c in range(out_ref.shape[1] // LANES):
        at = slice(c * share, (c + 1) * share)
        out_ref[:, c * LANES:(c + 1) * LANES] = e_ref[at, :] + drift_ref[at, :]


def call(body, name, outs, ins, scratch=()):
    return pl.pallas_call(
        body,
        out_shape=outs,
        in_specs=ins,
        out_specs=jax.tree.map(lambda _: VM, outs),
        scratch_shapes=scratch,
        compiler_params=PARAMS,
        name=name,
    )


def in_hbm(values):
    return pltpu.with_memory_space_constraint(values, pltpu.HBM)


def shape(*dims):
    return jax.ShapeDtypeStruct(dims, F32)


def shards(log_mean, tile_mask, coverage, lifetime, keep):
    rows, cols = log_mean.shape[1:]
    sections = keep.shape[0]
    parts = lax.axis_size("ta")
    share = cols // parts
    total = share + 2 * HALO
    used = rows * cols // LANES
    wide = -(-used // sections)
    padded = sections * wide
    turn = START % sections

    sent = call(
        lambda *refs: prepare_body(wide, turn, *refs),
        "prepare",
        shape(parts, total + 8, LANES),
        [HB] * 4,
        [pltpu.VMEM((rows, cols), a.dtype) for a in (log_mean, tile_mask, coverage, lifetime)]
        + [pltpu.VMEM((cols + 2 * HALO, LANES), F32), pltpu.VMEM((cols, LANES), F32)]
        + [pltpu.SemaphoreType.DMA((4,))],
    )(*(in_hbm(a) for a in (log_mean[0], tile_mask[0], coverage[0], lifetime)))
    ring = [(i + FIRST) % parts for i in range(parts)]
    sent = lax.all_to_all(sent, "ta", 0, 0, tiled=True, axis_index_groups=[ring])

    half = np.arange(rows * parts // 2)
    near = np.abs(half[:, None] - half[None, :]) <= RADIUS
    band = near.astype(BF16)
    edge = half.size // 2
    lane = np.arange(edge)
    source = np.tile(np.where(lane < edge // 2, lane + half.size, lane + edge), 2)
    target = half + edge
    joint = np.abs(source[:, None] - target[None, :]) <= RADIUS
    joint = joint & ((source < half.size)[:, None] != (target < half.size)[None, :])
    joint = joint.astype(BF16)
    smoothed, rest, life = call(
        lambda *refs: smooth_body(wide, turn, *refs),
        "smooth",
        (shape(padded, LANES), shape(used, LANES), shape(wide, LANES)),
        [VM] * 3,
        [pltpu.VMEM((total - 2 * RADIUS, rows * parts), F32)] * 2,
    )(sent, band, joint)

    order = [0] * sections
    for g in range(sections):
        order[seat_of(g, turn, sections)] = g

    def swap(values):
        flat = values.reshape(padded * LANES)
        flat = lax.all_to_all(flat, "gz", 0, 0, tiled=True, axis_index_groups=[order])
        return flat.reshape(padded, LANES)

    long = shape(padded, LANES)
    tables = call(
        norms_body,
        "norms",
        (shape(wide, LANES), long, long, long, long, shape(SPANS * wide, LANES)),
        [SM, VM],
    )(keep, life)
    drift = call(lambda *refs: scan_body(turn, *refs), "scan", long, [SM] + [VM] * 7)(
        keep, *tables, swap(smoothed)
    )
    out = call(finish_body, "finish", shape(share, rows * parts), [VM] * 2)(rest, swap(drift))
    return out.T[None]


def solution(mesh):
    return jax.shard_map(
        shards,
        mesh=mesh,
        in_specs=(
            P("gz", "ta", None),
            P("gz", "ta", None),
            P("gz", "ta", None),
            P("ta", None),
            P(),
        ),
        out_specs=P("gz", None, "ta"),
        check_vma=False,
    )
```

```python
import jax
import jax.numpy as jnp
import numpy as np
from jax import lax
from jax.experimental import pallas as pl
from jax.experimental.pallas import tpu as pltpu
from jax.sharding import PartitionSpec as P

RADIUS = 8
PASSES = 7
HALO = RADIUS * PASSES
START = 67
FIRST = 7
SPANS = 4
DEPTH = 12
LANES = 128
F32 = jnp.float32
BF16 = jnp.bfloat16
VM = pl.BlockSpec(memory_space=pltpu.VMEM)
HB = pl.BlockSpec(memory_space=pltpu.HBM)
SM = pl.BlockSpec(memory_space=pltpu.SMEM)
PARAMS = pltpu.CompilerParams(vmem_limit_bytes=16 << 20)


def seat_of(g, turn, sections):
    high = sections // DEPTH
    level = (g % DEPTH + DEPTH - turn % DEPTH) % DEPTH
    return level * high + (g // DEPTH + high - turn // DEPTH) % high


def prepare_body(
    wide, turn, log_hbm, mask_hbm, cov_hbm, life_hbm, out_ref,
    log_ref, mask_ref, cov_ref, life_ref, both_ref, life_t_ref, sems,
):
    pairs = ((life_hbm, life_ref), (log_hbm, log_ref), (mask_hbm, mask_ref), (cov_hbm, cov_ref))
    copies = [pltpu.make_async_copy(a, b, sems.at[i]) for i, (a, b) in enumerate(pairs)]
    for copy in copies:
        copy.start()
    rows, cols = log_ref.shape
    parts, depth, _ = out_ref.shape
    share = cols // parts
    span = share + 2 * HALO
    both_ref[:HALO, :] = jnp.zeros((HALO, LANES), F32)
    both_ref[HALO + cols:, :] = jnp.zeros((HALO, LANES), F32)
    copies[0].wait()
    life = jnp.concatenate([life_ref[...], life_ref[...]], axis=0)
    for c in range(0, cols, LANES):
        life_t_ref[c:c + LANES, :] = life[:, c:c + LANES].T
    for copy in copies[1:]:
        copy.wait()
    weight = 1.0 + mask_ref[...].astype(F32) * cov_ref[...].astype(F32)
    both = jnp.concatenate([weight, log_ref[...]], axis=0)
    for c in range(0, cols, LANES):
        both_ref[HALO + c:HALO + c + LANES, :] = both[:, c:c + LANES].T
    sections = lax.axis_size("gz")
    first = seat_of(lax.axis_index("gz"), turn, sections) * wide
    for t in range(parts):
        slot = (FIRST - t) % parts
        out_ref[slot, :span, :] = both_ref[share * t:share * t + span, :]
        out_ref[slot, span:, :] = jnp.zeros((depth - span, LANES), F32)
        for i in range(wide):
            place = share * t + (first + i) % share
            out_ref[slot, span + i:span + i + 1, :] = life_t_ref[pl.ds(place, 1), :]


def halves(values):
    high = values.astype(BF16)
    return high, (values - high.astype(F32)).astype(BF16)


def dot(a, b):
    return jnp.dot(a, b, preferred_element_type=F32)


def along_lanes(tiles, band, joint):
    values = jnp.concatenate(tiles, axis=0)
    rows = values.shape[0]
    half = band.shape[0]
    edge = half // 2
    both = jnp.concatenate(halves(values), axis=0)
    sides = dot(jnp.concatenate([both[:, :half], both[:, half:]], axis=0), band)
    left = sides[:rows] + sides[rows:2 * rows]
    right = sides[2 * rows:3 * rows] + sides[3 * rows:]
    near = lax.broadcasted_iota(jnp.int32, (rows, edge), 1) < edge // 2
    middle = jnp.where(near, values[:, half:half + edge], values[:, edge:half])
    across = dot(jnp.concatenate(halves(middle), axis=1), joint)
    sums = jnp.concatenate(
        [
            left[:, :edge],
            left[:, edge:] + across[:, :edge],
            right[:, :edge] + across[:, edge:],
            right[:, edge:],
        ],
        axis=1,
    )
    return [sums[r:r + 8] for r in range(0, rows, 8)]


def along_rows(tiles):
    count = len(tiles)
    row = lax.broadcasted_iota(jnp.int32, tiles[0].shape, 0)
    level = tiles
    for k in (1, 2, 4):
        turned = [pltpu.roll(v, 8 - k, 0) for v in level]
        after = turned[1:] + turned[-1:]
        level = [
            v + jnp.where(row < 8 - k, a, b) for v, a, b in zip(level, turned, after)
        ]
    return [level[j] + level[j + 1] + tiles[j + 2] for j in range(count - 2)]


def smooth_body(
    wide, turn, in_ref, band_ref, joint_ref, s_ref, e_ref, life_ref, inverse_ref, scale_ref
):
    parts = in_ref.shape[0]
    half = LANES // 2
    total = inverse_ref.shape[0] + 2 * RADIUS
    share = total - 2 * HALO
    left = lax.broadcasted_iota(jnp.int32, (total, LANES), 1) < half
    weights, fields = [], []
    for t in range(0, parts, 2):
        a = in_ref[(FIRST - t) % parts, :total, :]
        b = in_ref[(FIRST - t - 1) % parts, :total, :]
        weights.append(jnp.where(left, a, pltpu.roll(b, half, 1)))
        fields.append(jnp.where(left, pltpu.roll(a, half, 1), b))
    weight = jnp.concatenate(weights, axis=1)
    field = jnp.concatenate(fields, axis=1)

    sections = lax.axis_size("gz")
    first = seat_of(lax.axis_index("gz"), turn, sections) * wide
    left = lax.broadcasted_iota(jnp.int32, (1, LANES), 1) < half
    for i in range(wide):
        pair = 2 * jnp.minimum((first + i) // share, parts // 2 - 1)
        shift = parts + FIRST
        a = in_ref[lax.rem(shift - pair, parts), total + i:total + i + 1, :]
        b = in_ref[lax.rem(shift - pair - 1, parts), total + i:total + i + 1, :]
        life_ref[i:i + 1, :] = jnp.where(left, a, b)

    band = band_ref[...]
    joint = joint_ref[...]
    weights = [weight[r:r + 8] for r in range(0, total, 8)]
    now = [w * field[8 * j:8 * j + 8] for j, w in enumerate(weights)]
    denoms = along_rows(along_lanes(weights, band, joint))
    inverse = [1.0 / jnp.maximum(d, 1.0) for d in denoms]
    for j, value in enumerate(inverse):
        inverse_ref[8 * j:8 * j + 8, :] = value
        scale_ref[8 * j:8 * j + 8, :] = value * weights[j + 1]
    for level in range(PASSES):
        now = along_rows(along_lanes(now, band, joint))
        factor = scale_ref if level < PASSES - 1 else inverse_ref
        now = [
            v * factor[8 * (j + level):8 * (j + level + 1), :] for j, v in enumerate(now)
        ]
    smoothed = jnp.concatenate(now, axis=0)
    rest = field[HALO:HALO + share] - smoothed
    for c in range(parts // 2):
        s_ref[c * share:(c + 1) * share, :] = smoothed[:, c * LANES:(c + 1) * LANES]
        e_ref[c * share:(c + 1) * share, :] = rest[:, c * LANES:(c + 1) * LANES]
    used = e_ref.shape[0]
    s_ref[used:, :] = jnp.zeros((s_ref.shape[0] - used, LANES), F32)


def norms_body(
    keep_ref, life_ref, fade_ref, fore_ref, back_ref, fore_lead_ref, back_lead_ref, ends_ref
):
    sections = keep_ref.shape[0]
    wide = life_ref.shape[0]
    run = sections // SPANS
    fade = jnp.exp(-life_ref[...] / sections)
    fade_ref[...] = fade
    norm = jnp.zeros_like(fade)
    lead = jnp.ones_like(fade)
    for z in range(sections):
        at = slice(z * wide, (z + 1) * wide)
        decay = keep_ref[z] * fade
        gain = 1.0 - decay
        norm = decay * norm + gain
        lead = lead * decay if z % run else decay
        share = gain / norm
        fore_ref[at, :] = share
        fore_lead_ref[at, :] = lead * share
        if z % run == run - 1:
            ends_ref[z // run * wide:(z // run + 1) * wide, :] = lead
    norm = jnp.zeros_like(fade)
    for z in reversed(range(sections)):
        at = slice(z * wide, (z + 1) * wide)
        decay = keep_ref[z] * fade
        norm = decay * norm + (1.0 - decay)
        lead = lead * decay if (z + 1) % run else decay
        share = 1.0 / norm
        back_ref[at, :] = share
        back_lead_ref[at, :] = lead * share


def scan_body(
    turn, keep_ref, fade_ref, fore_ref, back_ref, fore_lead_ref, back_lead_ref, ends_ref,
    s_ref, out_ref,
):
    sections = keep_ref.shape[0]
    wide = fade_ref.shape[0]
    fade = fade_ref[...]
    run = sections // SPANS
    zero = jnp.zeros_like(fade)

    def rows(z):
        return slice(z * wide, (z + 1) * wide)

    def seat(z):
        return rows(seat_of(z, turn, sections))

    ends = [ends_ref[rows(k), :] for k in range(SPANS)]
    mass = [zero] * SPANS
    for i in range(run):
        for k in range(SPANS):
            z = k * run + i
            decay = keep_ref[z] * fade
            mass[k] = decay * mass[k] + (1.0 - decay) * s_ref[seat(z), :]
            out_ref[seat(z), :] = mass[k] * fore_ref[rows(z), :]
    carry = [zero]
    for k in range(SPANS - 1):
        carry.append(mass[k] + ends[k] * carry[k])
    mass = [zero] * SPANS
    for i in reversed(range(run)):
        for k in range(SPANS):
            z = k * run + i
            decay = keep_ref[z] * fade
            value = out_ref[seat(z), :] + fore_lead_ref[rows(z), :] * carry[k]
            mass[k] = decay * mass[k] + value
            out_ref[seat(z), :] = mass[k] * back_ref[rows(z), :]
    carry = [zero] * SPANS
    for k in reversed(range(SPANS - 1)):
        carry[k] = mass[k + 1] + ends[k + 1] * carry[k + 1]
    for k in range(SPANS - 1):
        for i in range(run):
            z = k * run + i
            out_ref[seat(z), :] = out_ref[seat(z), :] + back_lead_ref[rows(z), :] * carry[k]


def finish_body(e_ref, drift_ref, out_ref):
    share = out_ref.shape[0]
    for c in range(out_ref.shape[1] // LANES):
        at = slice(c * share, (c + 1) * share)
        out_ref[:, c * LANES:(c + 1) * LANES] = e_ref[at, :] + drift_ref[at, :]


def call(body, name, outs, ins, scratch=()):
    return pl.pallas_call(
        body,
        out_shape=outs,
        in_specs=ins,
        out_specs=jax.tree.map(lambda _: VM, outs),
        scratch_shapes=scratch,
        compiler_params=PARAMS,
        name=name,
    )


def in_hbm(values):
    return pltpu.with_memory_space_constraint(values, pltpu.HBM)


def shape(*dims):
    return jax.ShapeDtypeStruct(dims, F32)


def shards(log_mean, tile_mask, coverage, lifetime, keep):
    rows, cols = log_mean.shape[1:]
    sections = keep.shape[0]
    parts = lax.axis_size("ta")
    share = cols // parts
    total = share + 2 * HALO
    used = rows * cols // LANES
    wide = -(-used // sections)
    padded = sections * wide
    turn = START % sections

    sent = call(
        lambda *refs: prepare_body(wide, turn, *refs),
        "prepare",
        shape(parts, total + 8, LANES),
        [HB] * 4,
        [pltpu.VMEM((rows, cols), a.dtype) for a in (log_mean, tile_mask, coverage, lifetime)]
        + [pltpu.VMEM((cols + 2 * HALO, LANES), F32), pltpu.VMEM((cols, LANES), F32)]
        + [pltpu.SemaphoreType.DMA((4,))],
    )(*(in_hbm(a) for a in (log_mean[0], tile_mask[0], coverage[0], lifetime)))
    ring = [(FIRST - i) % parts for i in range(parts)]
    sent = lax.all_to_all(sent, "ta", 0, 0, tiled=True, axis_index_groups=[ring])

    half = np.arange(rows * parts // 2)
    near = np.abs(half[:, None] - half[None, :]) <= RADIUS
    band = near.astype(BF16)
    edge = half.size // 2
    lane = np.arange(edge)
    source = np.tile(np.where(lane < edge // 2, lane + half.size, lane + edge), 2)
    target = half + edge
    joint = np.abs(source[:, None] - target[None, :]) <= RADIUS
    joint = joint & ((source < half.size)[:, None] != (target < half.size)[None, :])
    joint = joint.astype(BF16)
    smoothed, rest, life = call(
        lambda *refs: smooth_body(wide, turn, *refs),
        "smooth",
        (shape(padded, LANES), shape(used, LANES), shape(wide, LANES)),
        [VM] * 3,
        [pltpu.VMEM((total - 2 * RADIUS, rows * parts), F32)] * 2,
    )(sent, band, joint)

    order = [0] * sections
    for g in range(sections):
        order[seat_of(g, turn, sections)] = g

    def swap(values):
        flat = values.reshape(padded * LANES)
        flat = lax.all_to_all(flat, "gz", 0, 0, tiled=True, axis_index_groups=[order])
        return flat.reshape(padded, LANES)

    long = shape(padded, LANES)
    tables = call(
        norms_body,
        "norms",
        (shape(wide, LANES), long, long, long, long, shape(SPANS * wide, LANES)),
        [SM, VM],
    )(keep, life)
    drift = call(lambda *refs: scan_body(turn, *refs), "scan", long, [SM] + [VM] * 7)(
        keep, *tables, swap(smoothed)
    )
    out = call(finish_body, "finish", shape(share, rows * parts), [VM] * 2)(rest, swap(drift))
    return out.T[None]


def solution(mesh):
    return jax.shard_map(
        shards,
        mesh=mesh,
        in_specs=(
            P("gz", "ta", None),
            P("gz", "ta", None),
            P("gz", "ta", None),
            P("ta", None),
            P(),
        ),
        out_specs=P("gz", None, "ta"),
        check_vma=False,
    )
```
